256 devices in a mesh: rows: 32 (over x, z_hi, core), mask: 8 (over z_lo, y).
Axes of the slice: x: 4, y: 4, z: 8 (z_hi: 4, z_lo: 2; z = z_hi * 2 + z_lo), core: 2. Of those that a mesh axis runs over, the one named last changes fastest.
Arguments:
- image_field: bfloat16 [2, 8192, 8192], P(None, ('rows', 'mask')), may hold values from -6 to 6
- amplitudes: bfloat16 [8, 8192, 8192], P('mask', None, 'rows'), may hold values from 0 to 12, as said below
- mask_ids: int32 [8], P('mask'), may hold values from 0 to 63
Outputs:
- gradient: float32 [2, 8192, 8192], P(None, ('rows', 'mask'))
- loss_value: float32 [], replicated
The draws below stay inside these ranges and needn't reach their ends.
Inputs may be any that keep to these rules, and one draw needn't show every extreme that they name: `amplitudes`: magnitudes are non-negative.
All inputs are finite; a program needn't handle non-finite values.
Results may differ from the reference program's by a relative error of at most 0.024.
Values may be sent and summed in bfloat16 or wider, within the bound.
A program may use at most 128 MiB of HBM per device.

```python
import math
import jax
import jax.numpy as jnp
from jax import lax

N = 8192
INNER = 128
MASK_SET = 64
M_WIN = 8


def draw_amplitudes(key, part):
    column_scale = 0.3 + 2.7 * jnp.arange(N, dtype=jnp.float32)[None, None, :] / N
    mask_scale = 0.6 + 0.8 * jnp.arange(M_WIN, dtype=jnp.float32)[:, None, None] / max(M_WIN - 1, 1)
    spread = jax.random.uniform(key, (M_WIN, N, N), jnp.float32, 0.2, 1.8)
    return (spread * column_scale * mask_scale).astype(jnp.bfloat16)


def place_ends(result, own_key, smallest, top_value):
    longest = result.shape.index(max(result.shape))
    spots = []
    for shift in (0, 1):
        where = [jax.random.randint(jax.random.fold_in(own_key, axis), (), 0, length) for axis, length in enumerate(result.shape)]
        where[longest] = (where[longest] + shift) % result.shape[longest]
        spots.append(tuple(where))
    return result.at[spots[0]].set(smallest).at[spots[1]].set(top_value)


def shard_levels(stream_key, shape, split, least, top_value):
    gain, own = 1.0, jax.random.fold_in(stream_key, 6)
    for dim, blocks in split:
        heights = jnp.exp(jax.random.uniform(jax.random.fold_in(own, dim), (blocks,), jnp.float32, least / len(split), top_value / len(split)))
        gain = gain * jnp.repeat(heights, shape[dim] // blocks).reshape([-1 if axis == dim else 1 for axis in range(len(shape))])
    return gain


def bell_draw(own_key, dims, deviation, most, shards=(), held_as=jnp.bfloat16):
    entries = jax.random.normal(own_key, dims, jnp.float32) * deviation
    if len(shards) > 0:
        entries = shard_levels(own_key, dims, shards, -0.22, 0.18) * entries
    return jnp.clip(entries, min=-most, max=most).astype(held_as)


def setup_inputs(seed: int = 0) -> dict:
    splits = jax.random.split(jax.random.key(seed), 4)
    return {
        "image_field": bell_draw(splits[0], (2, N, N), 1.0, 6.0, ((1, 256),)),
        "amplitudes": draw_amplitudes(jax.random.fold_in(splits[3], 71), 0),
        "mask_ids": place_ends(jax.random.randint(splits[2], (M_WIN,), 0, MASK_SET), jax.random.fold_in(splits[2], 1), 0, MASK_SET - 1).astype(jnp.int32),
    }


EPSILON = 0.25

def shift_bits(values, count):
    return lax.shift_right_logical(values, jnp.full(values.shape, count, jnp.int32))

def mask_code(window_id, row_index, column_index):
    mixed = row_index * jnp.int32(73856093) ^ column_index * jnp.int32(19349663) ^ (window_id + jnp.int32(1)) * jnp.int32(83492791)
    mixed = mixed ^ shift_bits(mixed, 13)
    mixed = mixed * jnp.int32(1274126177)
    mixed = mixed ^ shift_bits(mixed, 16)
    return shift_bits(mixed, 28) & jnp.int32(3)

def rotate(real_part, imag_part, phase_code, direction):
    cosine = (phase_code == 0).astype(jnp.float32) - (phase_code == 2).astype(jnp.float32)
    sine = direction * ((phase_code == 1).astype(jnp.float32) - (phase_code == 3).astype(jnp.float32))
    return (real_part * cosine - imag_part * sine, real_part * sine + imag_part * cosine)

def round_half(values):
    return lax.optimization_barrier(values.astype(jnp.bfloat16)).astype(jnp.float32)

def factor_table(length, direction):
    index = jnp.arange(length, dtype=jnp.int32)
    angles = (index[:, None] * index[None, :] % length).astype(jnp.float32) * (2.0 * math.pi / length)
    cosine = jnp.cos(angles)
    sine = direction * jnp.sin(angles)
    upper = jnp.stack([cosine, -sine], axis=1)
    lower = jnp.stack([sine, cosine], axis=1)
    return round_half(jnp.stack([upper, lower]))

def turn_table(outer, inner, length, direction):
    first = jnp.arange(outer, dtype=jnp.int32)[:, None]
    second = jnp.arange(inner, dtype=jnp.int32)[None, :]
    angles = (first * second % length).astype(jnp.float32) * (2.0 * math.pi / length)
    return (jnp.cos(angles), direction * jnp.sin(angles))

def factor(form, table, values):
    return jnp.einsum(form, table.astype(jnp.float32), values.astype(jnp.float32), precision=lax.Precision.HIGHEST)

def twist(real_part, imag_part, cosine, sine, axis):
    return round_half(jnp.stack([real_part * cosine - imag_part * sine, real_part * sine + imag_part * cosine], axis=axis))

def rows_forward(values, tables):
    lead_table, sub_table, cosine, sine = tables
    batch, parts, count, length = values.shape
    view = values.reshape(batch, parts, count, lead_table.shape[1], sub_table.shape[1])
    first = factor('pkqj,xqrjb->xprkb', lead_table, view)
    middle = twist(first[:, 0], first[:, 1], cosine, sine, 1)
    second = factor('pkqj,xqraj->xprak', sub_table, middle)
    return second.reshape(batch, parts, count, length) * (1.0 / math.sqrt(length))

def rows_inverse(values, tables):
    lead_table, sub_table, cosine, sine = tables
    batch, parts, count, length = values.shape
    view = values.reshape(batch, parts, count, lead_table.shape[1], sub_table.shape[1])
    first = factor('pkqj,xqraj->xprak', sub_table, view)
    middle = twist(first[:, 0], first[:, 1], cosine, sine, 1)
    second = factor('pkqj,xqrjb->xprkb', lead_table, middle)
    return second.reshape(batch, parts, count, length) * (1.0 / math.sqrt(length))

def cols_forward(values, tables):
    lead_table, sub_table, cosine, sine = tables
    parts, length, width = values.shape
    view = values.reshape(parts, lead_table.shape[1], sub_table.shape[1], width)
    first = factor('pkqj,qjbw->pkbw', lead_table, view)
    middle = twist(first[0], first[1], cosine[:, :, None], sine[:, :, None], 0)
    second = factor('pkqj,qajw->pakw', sub_table, middle)
    return second.reshape(parts, length, width) * (1.0 / math.sqrt(length))

def cols_inverse(values, tables):
    lead_table, sub_table, cosine, sine = tables
    parts, length, width = values.shape
    view = values.reshape(parts, lead_table.shape[1], sub_table.shape[1], width)
    first = factor('pkqj,qajw->pakw', sub_table, view)
    middle = twist(first[0], first[1], cosine[:, :, None], sine[:, :, None], 0)
    second = factor('pkqj,qjbw->pkbw', lead_table, middle)
    return second.reshape(parts, length, width) * (1.0 / math.sqrt(length))

def reference(image_field, amplitudes, mask_ids):
    outer = N // INNER
    forward_cos, forward_sin = turn_table(outer, INNER, N, -1.0)
    inverse_cos, inverse_sin = turn_table(outer, INNER, N, 1.0)
    forward_tables = (factor_table(outer, -1.0), factor_table(INNER, -1.0), forward_cos, forward_sin)
    inverse_tables = (factor_table(outer, 1.0), factor_table(INNER, 1.0), inverse_cos, inverse_sin)
    row_index = jnp.arange(N, dtype=jnp.int32)[:, None]
    column_index = jnp.arange(N, dtype=jnp.int32)[None, :]
    field_real = image_field[0].astype(jnp.float32)
    field_imag = image_field[1].astype(jnp.float32)
    grad_real = jnp.zeros((N, N), jnp.float32)
    grad_imag = jnp.zeros((N, N), jnp.float32)
    loss_sum = jnp.zeros((), jnp.float32)
    for which in range(M_WIN):
        phase_code = mask_code(mask_ids[which], row_index, column_index)
        masked_real, masked_imag = rotate(field_real, field_imag, phase_code, 1.0)
        masked = round_half(jnp.stack([masked_real, masked_imag]))
        sent = round_half(rows_forward(masked[None], forward_tables)[0])
        spectrum = cols_forward(sent, forward_tables)
        spec_real = spectrum[0]
        spec_imag = spectrum[1]
        measured = amplitudes[which].astype(jnp.float32)
        magnitude = jnp.sqrt(spec_real * spec_real + spec_imag * spec_imag + EPSILON)
        factor_kept = 1.0 - measured / magnitude
        misfit = magnitude - measured
        loss_sum = loss_sum + jnp.sum(misfit * misfit)
        weighted = round_half(jnp.stack([spec_real * factor_kept, spec_imag * factor_kept]))
        columns_back = round_half(cols_inverse(weighted, inverse_tables))
        rows_back = rows_inverse(columns_back[None], inverse_tables)[0]
        term_real, term_imag = rotate(rows_back[0], rows_back[1], phase_code, -1.0)
        grad_real = grad_real + round_half(term_real)
        grad_imag = grad_imag + round_half(term_imag)
    gradient = jnp.stack([grad_real, grad_imag])
    return (gradient, loss_sum / (M_WIN * N * N))
```

```python
import functools
import math

import jax
import jax.numpy as jnp
import ml_dtypes
import numpy as np
from jax import lax
from jax.experimental import pallas as pl
from jax.experimental.pallas import tpu as pltpu
from jax.sharding import Mesh
from jax.sharding import PartitionSpec as P

N = 8192
LEAD = 64
SUB = 128
SLAB = 32
STRIDE = 136
EPSILON = 0.25
CHUNKS = 2
ROW_PRIME, COLUMN_PRIME, MASK_PRIME, MIX_PRIME = 73856093, 19349663, 83492791, 1274126177
BF16 = jnp.bfloat16
F32 = jnp.float32


def rounded(values):
    return values.astype(ml_dtypes.bfloat16).astype(np.float32)


def unit_table(outputs, inputs, length, direction):
    angles = (outputs[:, None] * inputs[None, :] % length) * (2.0 * math.pi / length)
    return np.cos(angles), direction * np.sin(angles)


def block_form(real_part, imag_part):
    return np.block([[real_part, -imag_part], [imag_part, real_part]])


def orders():
    x, core, jh, b = np.meshgrid(np.arange(4), np.arange(2), np.arange(2), np.arange(4), indexing="ij")
    k1 = (x * 16 + b * 4 + core * 2 + jh).reshape(-1)
    x, core, zh, zl = np.meshgrid(np.arange(4), np.arange(2), np.arange(4), np.arange(2), indexing="ij")
    n1 = (x * 16 + zh * 4 + core * 2 + zl).reshape(-1)
    return k1, n1


def tables():
    k1_order, n1_order = orders()
    lead, sub = np.arange(LEAD), np.arange(SUB)
    out = {}
    lanes = np.arange(256)
    half, part, low = lanes // 128, (lanes // 64) % 2, lanes % 64
    split = part * 128 + half * 64 + low
    for name, direction in (("forward", -1.0), ("inverse", 1.0)):
        sub_full = block_form(*map(rounded, unit_table(sub, sub, SUB, direction)))
        out[name + "_sub"] = sub_full.astype(ml_dtypes.bfloat16)
        if name == "forward":
            row_lead = block_form(*map(rounded, unit_table(k1_order, lead, LEAD, direction)))
            row_sub = sub_full.T[:, split]
            turn = unit_table(k1_order, sub, N, direction)
            col = tuple(map(rounded, unit_table(lead, n1_order, LEAD, direction)))
        else:
            row_lead = block_form(*map(rounded, unit_table(lead, k1_order, LEAD, direction)))
            row_sub = sub_full.T[split, :]
            turn = tuple(np.repeat(t, 8, axis=0) for t in unit_table(k1_order, sub, N, direction))
            col = tuple(map(rounded, unit_table(n1_order, lead, LEAD, direction)))
        out[name + "_row_lead"] = row_lead.astype(ml_dtypes.bfloat16)
        out[name + "_row_sub"] = row_sub.astype(ml_dtypes.bfloat16)
        out[name + "_turn"] = np.stack(turn).astype(np.float32)
        col_plain = block_form(*col).astype(np.float32)
        col_quarter = block_form(-col[1], col[0]).astype(np.float32)
        out[name + "_col"] = np.stack([col_plain, col_quarter])
        twist = unit_table(sub, np.concatenate([lead, lead]), N, direction)
        out[name + "_col_turn"] = np.stack(twist).astype(np.float32)
    return out


def column_tables(table, name):
    plain, quarter = table[name + "_col"]
    cosine, sine = table[name + "_col_turn"]
    plain, quarter, cosine, sine = map(jnp.asarray, (plain, quarter, cosine, sine))
    if name == "forward":
        cosine, sine = cosine[:, :, None], sine[:, :, None]
    else:
        cosine, sine = cosine[:, None, :], sine[:, None, :]
    return (plain[None] * cosine + quarter[None] * sine).astype(BF16)


def phase_code(hashed_columns, row_term):
    mixed = hashed_columns ^ row_term
    mixed = mixed ^ lax.shift_right_logical(mixed, jnp.int32(13))
    mixed = mixed * jnp.int32(MIX_PRIME)
    mixed = mixed ^ lax.shift_right_logical(mixed, jnp.int32(16))
    return lax.shift_right_logical(mixed, jnp.int32(28))


def column_hash():
    shape = (LEAD, SUB)
    column = lax.broadcasted_iota(jnp.int32, shape, 0) * SUB + lax.broadcasted_iota(jnp.int32, shape, 1)
    return column * jnp.int32(COLUMN_PRIME)


def quarter_turn(real_part, imag_part, code, forward):
    odd = (code & 1) == 1
    first = jnp.where(odd, imag_part, real_part)
    second = jnp.where(odd, real_part, imag_part)
    high = (code & 2) == 2
    mixed = ((code ^ lax.shift_right_logical(code, jnp.int32(1))) & 1) == 1
    flip_real, flip_imag = (mixed, high) if forward else (high, mixed)
    return jnp.where(flip_real, -first, first), jnp.where(flip_imag, -second, second)


def row_forward_kernel(first_row, scalars, image, lead_table, sub_table, turn, out, swap):
    count = image.shape[2]
    columns = column_hash()

    def body(r, carry):
        stacked = []
        for zs in range(8):
            row = scalars[zs] + first_row + r
            code = phase_code(columns, (row * jnp.int32(ROW_PRIME)) ^ scalars[8])
            real_part, imag_part = image[zs, 0, r].astype(F32), image[zs, 1, r].astype(F32)
            real_part, imag_part = quarter_turn(real_part, imag_part, code, True)
            stacked.append(jnp.concatenate([real_part, imag_part], axis=0).astype(BF16))
        first = jnp.dot(lead_table[...], jnp.concatenate(stacked, axis=1), preferred_element_type=F32)
        cosine, sine = turn[0], turn[1]
        middle = []
        for zs in range(8):
            real_part, imag_part = first[:LEAD, zs * 128 : zs * 128 + 128], first[LEAD:, zs * 128 : zs * 128 + 128]
            turned = [real_part * cosine - imag_part * sine, real_part * sine + imag_part * cosine]
            middle.append(jnp.concatenate(turned, axis=1).astype(BF16))
        second = jnp.dot(jnp.concatenate(middle, axis=0), sub_table[...], preferred_element_type=F32)
        for zs in range(8):
            for half in range(2):
                swap[half, pl.ds(zs, LEAD, stride=8), :] = second[zs * LEAD : (zs + 1) * LEAD, half * 128 : half * 128 + 128]
        for x in range(4):
            for core in range(2):
                for jh in range(2):
                    at = ((x * 2 + core) * 2 + jh) * 32
                    for half in range(2):
                        out[(x * 4 + jh * 2 + half) * 2 + core, r] = swap[half, at : at + 32, :].astype(BF16)
        return carry

    lax.fori_loop(0, count, body, 0)


def row_inverse_kernel(first_row, scalars, field, lead_table, sub_table, turn, out, swap):
    count = field.shape[1]
    columns = column_hash()

    def body(r, carry):
        blocks = []
        for x in range(4):
            for core in range(2):
                for jh in range(2):
                    pair = [field[(x * 4 + jh * 2 + half) * 2 + core, r] for half in range(2)]
                    blocks.append(jnp.concatenate(pair, axis=1))
        first = jnp.dot(jnp.concatenate(blocks, axis=0), sub_table[...], preferred_element_type=F32)
        real_part, imag_part = first[:, :128], first[:, 128:]
        cosine, sine = turn[0], turn[1]
        swap[0] = real_part * cosine - imag_part * sine
        swap[1] = real_part * sine + imag_part * cosine
        middle = []
        for zs in range(8):
            parts = [swap[part, pl.ds(zs, LEAD, stride=8), :] for part in range(2)]
            middle.append(jnp.concatenate(parts, axis=0).astype(BF16))
        second = jnp.dot(lead_table[...], jnp.concatenate(middle, axis=1), preferred_element_type=F32)
        second = second * (1.0 / N)
        for zs in range(8):
            row = scalars[zs] + first_row + r
            code = phase_code(columns, (row * jnp.int32(ROW_PRIME)) ^ scalars[8])
            real_part, imag_part = second[:LEAD, zs * 128 : zs * 128 + 128], second[LEAD:, zs * 128 : zs * 128 + 128]
            real_part, imag_part = quarter_turn(real_part, imag_part, code, False)
            out[zs, 0, r] = real_part.astype(BF16)
            out[zs, 1, r] = imag_part.astype(BF16)
        return carry

    lax.fori_loop(0, count, body, 0)


def pair_up(first, second, low):
    return jnp.where(low, first, pltpu.roll(second, 64, 1)), jnp.where(low, pltpu.roll(first, 64, 1), second)


def pack_kernel(place, amplitudes, *outs):
    for shift, out in enumerate(outs):
        piece = lax.rem(place[0] + shift, 4)
        lanes = pl.ds(pl.multiple_of(piece // 2 * 128, 128), 128)
        upper, lower = amplitudes[0, :, lanes].astype(F32), amplitudes[1, :, lanes].astype(F32)
        low = lax.broadcasted_iota(jnp.int32, upper.shape, 1) < 64
        left, right = pair_up(upper, lower, low)
        out[...] = jnp.where(lax.rem(piece, 2) == 0, left, right).astype(BF16)


def column_kernel(*refs):
    fields = refs[:CHUNKS]
    place, amplitudes, forward_lead, inverse_lead, forward_sub, inverse_sub = refs[CHUNKS : CHUNKS + 6]
    outs = refs[CHUNKS + 6 : 2 * CHUNKS + 6]
    loss, hold = refs[2 * CHUNKS + 6 :]
    count = SLAB // CHUNKS

    for chunk in range(CHUNKS):

        def forward(step, carry, chunk=chunk):
            y, r = step // count, lax.rem(step, count)
            at = y * SLAB + chunk * count + r
            low = lax.broadcasted_iota(jnp.int32, (8, 128), 1) < 64
            parts = [[[], []], [[], []]]
            for x in range(4):
                for core in range(2):
                    block = fields[chunk][(x * 4 + y) * 2 + core, r].astype(F32)
                    for pair in range(2):
                        real_part, imag_part = pair_up(block[pair * 16 : pair * 16 + 8], block[pair * 16 + 8 : pair * 16 + 16], low)
                        parts[0][pair].append(real_part)
                        parts[1][pair].append(imag_part)
            stacked = jnp.concatenate(
                [jnp.concatenate([jnp.concatenate(parts[part][pair], axis=0) for pair in range(2)], axis=1) for part in range(2)], axis=0
            ).astype(BF16)
            result = jnp.dot(forward_lead[at], stacked, preferred_element_type=F32)
            for part in range(2):
                for pair in range(2):
                    hold[part, pair, pl.ds(at, LEAD, stride=STRIDE), :] = result[part * 64 : part * 64 + 64, pair * 128 : pair * 128 + 128]
            return carry

        lax.fori_loop(0, 4 * count, forward, 0, unroll=8)

    loss[...] = jnp.zeros_like(loss)

    def middle(k1_low, carry):
        low = lax.broadcasted_iota(jnp.int32, (SUB, 128), 1) < 64
        measured = [[], []]
        for pair in range(2):
            first, second = (amplitudes[lax.rem(place[0] + 4 - b, 4), k1_low].astype(F32) for b in (pair * 2, pair * 2 + 1))
            for high, values in enumerate(pair_up(first, second, low)):
                measured[high].append(values)
        places = [pl.ds(pl.multiple_of((k1_low + high * 32) * STRIDE, 8), SUB) for high in range(2)]
        stacked = [
            jnp.concatenate(
                [jnp.concatenate([hold[part, pair, at, :].astype(BF16) for pair in range(2)], axis=1) for part in range(2)], axis=0
            )
            for at in places
        ]
        spectra = [jnp.dot(forward_sub[...], values, preferred_element_type=F32) for values in stacked]
        weighted, total = [], 0.0
        for spectrum, values in zip(spectra, measured):
            real_part, imag_part = spectrum[:SUB] * (1.0 / N), spectrum[SUB:] * (1.0 / N)
            amplitude = jnp.concatenate(values, axis=1)
            squared = real_part * real_part + imag_part * imag_part + EPSILON
            inverse = lax.rsqrt(squared)
            kept = 1.0 - amplitude * inverse
            misfit = squared * inverse - amplitude
            total = total + jnp.sum((misfit * misfit).reshape(SUB // 8, 8, 256), axis=0)
            weighted.append(jnp.concatenate([(real_part * kept).astype(BF16), (imag_part * kept).astype(BF16)], axis=0))
        results = [jnp.dot(inverse_sub[...], values, preferred_element_type=F32) for values in weighted]
        loss[...] += total
        for at, result in zip(places, results):
            for part in range(2):
                for pair in range(2):
                    hold[part, pair, at, :] = result[part * SUB : part * SUB + SUB, pair * 128 : pair * 128 + 128]
        return carry

    lax.fori_loop(0, 32, middle, 0, unroll=2)

    for chunk in range(CHUNKS):

        def inverse(step, carry, chunk=chunk):
            y, r = step // count, lax.rem(step, count)
            at = y * SLAB + chunk * count + r
            low = lax.broadcasted_iota(jnp.int32, (8, 128), 1) < 64
            stacked = jnp.concatenate(
                [jnp.concatenate([hold[part, pair, pl.ds(at, LEAD, stride=STRIDE), :] for pair in range(2)], axis=1) for part in range(2)],
                axis=0,
            ).astype(BF16)
            result = jnp.dot(inverse_lead[at], stacked, preferred_element_type=F32)
            for x in range(4):
                for core in range(2):
                    row = (x * 2 + core) * 8
                    block = []
                    for pair in range(2):
                        real_part = result[row : row + 8, pair * 128 : pair * 128 + 128]
                        imag_part = result[64 + row : 64 + row + 8, pair * 128 : pair * 128 + 128]
                        block.extend(pair_up(real_part, imag_part, low))
                    outs[chunk][(x * 4 + y) * 2 + core, r] = jnp.concatenate(block, axis=0).astype(BF16)
            return carry

        lax.fori_loop(0, 4 * count, inverse, 0, unroll=8)


VMEM = pl.BlockSpec(memory_space=pltpu.VMEM)
SMEM = pl.BlockSpec(memory_space=pltpu.SMEM)


def params(mib):
    return pltpu.CompilerParams(vmem_limit_bytes=mib * 2**20)


def cost(flops, moved):
    return pl.CostEstimate(flops=flops, bytes_accessed=moved, transcendentals=0)


def row_forward(table, first_row, scalars, image):
    count = image.shape[2]
    return pl.pallas_call(
        functools.partial(row_forward_kernel, first_row),
        out_shape=jax.ShapeDtypeStruct((32, count, 32, 128), BF16),
        in_specs=[SMEM] + [VMEM] * 4,
        out_specs=VMEM,
        scratch_shapes=[pltpu.VMEM((2, 512, 128), F32)],
        compiler_params=params(40),
        cost_estimate=cost(count * 10**9, count * 2**19),
        name="row_forward",
    )(scalars, image, table["forward_row_lead"], table["forward_row_sub"], table["forward_turn"])


def row_inverse(table, first_row, scalars, field):
    count = field.shape[1]
    return pl.pallas_call(
        functools.partial(row_inverse_kernel, first_row),
        out_shape=jax.ShapeDtypeStruct((8, 2, count, LEAD, SUB), BF16),
        in_specs=[SMEM] + [VMEM] * 4,
        out_specs=VMEM,
        scratch_shapes=[pltpu.VMEM((2, 512, 128), F32)],
        compiler_params=params(40),
        cost_estimate=cost(count * 10**9, count * 2**19),
        name="row_inverse",
    )(scalars, field, table["inverse_row_lead"], table["inverse_row_sub"], table["inverse_turn"])


def pack(place, amplitudes):
    rows = N // 2
    step = 512
    return pl.pallas_call(
        pack_kernel,
        grid=(rows // step,),
        out_shape=[jax.ShapeDtypeStruct((rows, 128), BF16)] * 4,
        in_specs=[SMEM, pl.BlockSpec((2, step, 256), lambda i: (0, i, 0))],
        out_specs=[pl.BlockSpec((step, 128), lambda i: (i, 0))] * 4,
        cost_estimate=cost(10**7, 2**23),
        name="pack",
    )(place, amplitudes.reshape(2, rows, 256))


def columns(table, fields, place, amplitudes, forward_lead, inverse_lead):
    count = SLAB // CHUNKS
    result = pl.pallas_call(
        column_kernel,
        out_shape=[jax.ShapeDtypeStruct((32, count, 32, 128), BF16)] * CHUNKS + [jax.ShapeDtypeStruct((8, 256), F32)],
        in_specs=[VMEM] * CHUNKS + [SMEM] + [VMEM] * 5,
        out_specs=[VMEM] * (CHUNKS + 1),
        scratch_shapes=[pltpu.VMEM((2, 2, LEAD * STRIDE, 128), F32)],
        compiler_params=params(58),
        cost_estimate=cost(40 * 10**9, 2**25),
        name="columns",
    )(*fields, place, amplitudes, forward_lead, inverse_lead, table["forward_sub"], table["inverse_sub"])
    return result[:-1], result[-1]


def shift_by(piece, axis, shift):
    return piece if shift == 0 else lax.ppermute(piece, axis, [(i, (i + shift) % 4) for i in range(4)])


def fold(value, axis, distance):
    return value + lax.ppermute(value, axis, [(i, i ^ distance) for i in range(lax.axis_size(axis))])


def shards(table, image_field, amplitudes, mask_ids):
    plane = ("x", "y", "core")
    x, zh, core, zl, y = (lax.axis_index(name) for name in ("x", "zh", "core", "zl", "y"))
    swap = [(a * 4 + b, b * 4 + a) for a in range(4) for b in range(4)]
    mask_term = (lax.ppermute(mask_ids, ("zh", "y"), swap) + 1) * jnp.int32(MASK_PRIME)
    zs = jnp.arange(8, dtype=jnp.int32)
    first_rows = (((x * 4 + zs // 2) * 2 + core) * 8 + zs % 2 * 4 + y) * SLAB
    scalars = jnp.concatenate([first_rows.astype(jnp.int32), mask_term])
    count = SLAB // CHUNKS

    image = image_field.reshape(2, SLAB, LEAD, SUB)
    slabs = [lax.all_gather(image[:, c * count : (c + 1) * count], ("zh", "zl"), axis=0) for c in range(CHUNKS)]

    packed = pack(y[None].astype(jnp.int32), amplitudes)
    spread = [shift_by(piece, "y", s) for s, piece in enumerate(packed)]
    spread, slabs[0] = lax.optimization_barrier((spread, slabs[0]))
    spread = jnp.stack(spread)
    sent = [row_forward(table, 0, scalars, slabs[0])]
    fields = [lax.all_to_all(sent[0], plane, 0, 0, tiled=True)]
    spread, slabs[-1], fields[0] = lax.optimization_barrier((spread, slabs[-1], fields[0]))
    packed = [lax.dynamic_index_in_dim(spread, lax.rem(y - zh - t + 8, 4), 0, False) for t in range(4)]
    packed = jnp.stack([shift_by(piece, "zh", t) for t, piece in enumerate(packed)])
    packed = packed.reshape(4, 32, SUB, 128)
    forward_lead = column_tables(table, "forward")
    inverse_lead = column_tables(table, "inverse")
    sent.extend(row_forward(table, c * count, scalars, slabs[c]) for c in range(1, CHUNKS))
    fields.extend(lax.all_to_all(piece, plane, 0, 0, tiled=True) for piece in sent[1:])
    returned, loss = columns(table, fields, zh[None].astype(jnp.int32), packed, forward_lead, inverse_lead)
    loss_total = jnp.sum(loss).reshape(1)
    for axis, distance in (("zl", 1), ("zh", 1), ("zh", 2), ("core", 1), ("x", 1), ("x", 2), ("y", 1), ("y", 2)):
        loss_total = fold(loss_total, axis, distance)
    pieces = []
    returned = list(returned)
    for c in range(CHUNKS):
        back = lax.all_to_all(returned[c], plane, 0, 0, tiled=True)
        if c == 0:
            loss_total, back, returned[1:] = lax.optimization_barrier((loss_total, back, returned[1:]))
        term = row_inverse(table, c * count, scalars, back)
        pieces.append(lax.psum_scatter(term, ("zh", "zl"), scatter_dimension=0, tiled=False))
    gradient = jnp.concatenate(pieces, axis=1).astype(F32).reshape(2, SLAB, N)
    return gradient, loss_total[0] / (8 * N * N)


def solution(mesh):
    fine = Mesh(mesh.devices.reshape(4, 4, 2, 2, 4), ("x", "zh", "core", "zl", "y"))
    rows, mask = ("x", "zh", "core"), ("zl", "y")
    return jax.shard_map(
        functools.partial(shards, tables()),
        mesh=fine,
        in_specs=(P(None, rows + mask, None), P(mask, None, rows), P(mask)),
        out_specs=(P(None, rows + mask, None), P()),
        check_vma=False,
    )
```

```python
import functools
import math

import jax
import jax.numpy as jnp
import ml_dtypes
import numpy as np
from jax import lax
from jax.experimental import pallas as pl
from jax.experimental.pallas import tpu as pltpu
from jax.sharding import Mesh
from jax.sharding import PartitionSpec as P

N = 8192
LEAD = 64
SUB = 128
SLAB = 32
STRIDE = 136
EPSILON = 0.25
CHUNKS = 2
EARLY = 1280
ROW_PRIME, COLUMN_PRIME, MASK_PRIME, MIX_PRIME = 73856093, 19349663, 83492791, 1274126177
BF16 = jnp.bfloat16
F32 = jnp.float32


def rounded(values):
    return values.astype(ml_dtypes.bfloat16).astype(np.float32)


def unit_table(outputs, inputs, length, direction):
    angles = (outputs[:, None] * inputs[None, :] % length) * (2.0 * math.pi / length)
    return np.cos(angles), direction * np.sin(angles)


def block_form(real_part, imag_part):
    return np.block([[real_part, -imag_part], [imag_part, real_part]])


def orders():
    x, core, jh, b = np.meshgrid(np.arange(4), np.arange(2), np.arange(2), np.arange(4), indexing="ij")
    k1 = (x * 16 + b * 4 + core * 2 + jh).reshape(-1)
    x, core, zh, zl = np.meshgrid(np.arange(4), np.arange(2), np.arange(4), np.arange(2), indexing="ij")
    n1 = (x * 16 + zh * 4 + core * 2 + zl).reshape(-1)
    return k1, n1


def tables():
    k1_order, n1_order = orders()
    lead, sub = np.arange(LEAD), np.arange(SUB)
    out = {}
    lanes = np.arange(256)
    half, part, low = lanes // 128, (lanes // 64) % 2, lanes % 64
    split = part * 128 + half * 64 + low
    for name, direction in (("forward", -1.0), ("inverse", 1.0)):
        sub_full = block_form(*map(rounded, unit_table(sub, sub, SUB, direction)))
        out[name + "_sub"] = sub_full.astype(ml_dtypes.bfloat16)
        if name == "forward":
            row_lead = block_form(*map(rounded, unit_table(k1_order, lead, LEAD, direction)))
            row_sub = sub_full.T[:, split]
            turn = unit_table(k1_order, sub, N, direction)
            col = tuple(map(rounded, unit_table(lead, n1_order, LEAD, direction)))
        else:
            row_lead = block_form(*map(rounded, unit_table(lead, k1_order, LEAD, direction)))
            row_sub = sub_full.T[split, :]
            turn = tuple(np.repeat(t, 8, axis=0) for t in unit_table(k1_order, sub, N, direction))
            col = tuple(map(rounded, unit_table(n1_order, lead, LEAD, direction)))
        out[name + "_row_lead"] = row_lead.astype(ml_dtypes.bfloat16)
        out[name + "_row_sub"] = row_sub.astype(ml_dtypes.bfloat16)
        out[name + "_turn"] = np.stack(turn).astype(np.float32)
        col_plain = block_form(*col).astype(np.float32)
        col_quarter = block_form(-col[1], col[0]).astype(np.float32)
        out[name + "_col"] = np.stack([col_plain, col_quarter])
        twist = unit_table(sub, np.concatenate([lead, lead]), N, direction)
        out[name + "_col_turn"] = np.stack(twist).astype(np.float32)
    return out


def column_tables(table, name):
    plain, quarter = table[name + "_col"]
    cosine, sine = table[name + "_col_turn"]
    plain, quarter, cosine, sine = map(jnp.asarray, (plain, quarter, cosine, sine))
    if name == "forward":
        cosine, sine = cosine[:, :, None], sine[:, :, None]
    else:
        cosine, sine = cosine[:, None, :], sine[:, None, :]
    return (plain[None] * cosine + quarter[None] * sine).astype(BF16)


def phase_code(hashed_columns, row_term):
    mixed = hashed_columns ^ row_term
    mixed = mixed ^ lax.shift_right_logical(mixed, jnp.int32(13))
    mixed = mixed * jnp.int32(MIX_PRIME)
    mixed = mixed ^ lax.shift_right_logical(mixed, jnp.int32(16))
    return lax.shift_right_logical(mixed, jnp.int32(28))


def column_hash():
    shape = (LEAD, SUB)
    column = lax.broadcasted_iota(jnp.int32, shape, 0) * SUB + lax.broadcasted_iota(jnp.int32, shape, 1)
    return column * jnp.int32(COLUMN_PRIME)


def quarter_turn(real_part, imag_part, code, forward):
    odd = (code & 1) == 1
    first = jnp.where(odd, imag_part, real_part)
    second = jnp.where(odd, real_part, imag_part)
    high = (code & 2) == 2
    mixed = ((code ^ lax.shift_right_logical(code, jnp.int32(1))) & 1) == 1
    flip_real, flip_imag = (mixed, high) if forward else (high, mixed)
    return jnp.where(flip_real, -first, first), jnp.where(flip_imag, -second, second)


def row_forward_kernel(first_row, scalars, image, lead_table, sub_table, turn, out, swap):
    count = image.shape[2]
    columns = column_hash()

    def body(r, carry):
        stacked = []
        for zs in range(8):
            row = scalars[zs] + first_row + r
            code = phase_code(columns, (row * jnp.int32(ROW_PRIME)) ^ scalars[8])
            real_part, imag_part = image[zs, 0, r].astype(F32), image[zs, 1, r].astype(F32)
            real_part, imag_part = quarter_turn(real_part, imag_part, code, True)
            stacked.append(jnp.concatenate([real_part, imag_part], axis=0).astype(BF16))
        first = jnp.dot(lead_table[...], jnp.concatenate(stacked, axis=1), preferred_element_type=F32)
        cosine, sine = turn[0], turn[1]
        middle = []
        for zs in range(8):
            real_part, imag_part = first[:LEAD, zs * 128 : zs * 128 + 128], first[LEAD:, zs * 128 : zs * 128 + 128]
            turned = [real_part * cosine - imag_part * sine, real_part * sine + imag_part * cosine]
            middle.append(jnp.concatenate(turned, axis=1).astype(BF16))
        second = jnp.dot(jnp.concatenate(middle, axis=0), sub_table[...], preferred_element_type=F32)
        for zs in range(8):
            for half in range(2):
                swap[half, pl.ds(zs, LEAD, stride=8), :] = second[zs * LEAD : (zs + 1) * LEAD, half * 128 : half * 128 + 128]
        for x in range(4):
            for core in range(2):
                for jh in range(2):
                    at = ((x * 2 + core) * 2 + jh) * 32
                    for half in range(2):
                        out[(x * 4 + jh * 2 + half) * 2 + core, r] = swap[half, at : at + 32, :].astype(BF16)
        return carry

    lax.fori_loop(0, count, body, 0, unroll=4)


def row_inverse_kernel(first_row, scalars, field, lead_table, sub_table, turn, out, swap):
    count = field.shape[1]
    columns = column_hash()

    def body(r, carry):
        blocks = []
        for x in range(4):
            for core in range(2):
                for jh in range(2):
                    pair = [field[(x * 4 + jh * 2 + half) * 2 + core, r] for half in range(2)]
                    blocks.append(jnp.concatenate(pair, axis=1))
        first = jnp.dot(jnp.concatenate(blocks, axis=0), sub_table[...], preferred_element_type=F32)
        real_part, imag_part = first[:, :128], first[:, 128:]
        cosine, sine = turn[0], turn[1]
        swap[0] = real_part * cosine - imag_part * sine
        swap[1] = real_part * sine + imag_part * cosine
        middle = []
        for zs in range(8):
            parts = [swap[part, pl.ds(zs, LEAD, stride=8), :] for part in range(2)]
            middle.append(jnp.concatenate(parts, axis=0).astype(BF16))
        second = jnp.dot(lead_table[...], jnp.concatenate(middle, axis=1), preferred_element_type=F32)
        second = second * (1.0 / N)
        for zs in range(8):
            row = scalars[zs] + first_row + r
            code = phase_code(columns, (row * jnp.int32(ROW_PRIME)) ^ scalars[8])
            real_part, imag_part = second[:LEAD, zs * 128 : zs * 128 + 128], second[LEAD:, zs * 128 : zs * 128 + 128]
            real_part, imag_part = quarter_turn(real_part, imag_part, code, False)
            out[zs, 0, r] = real_part.astype(BF16)
            out[zs, 1, r] = imag_part.astype(BF16)
        return carry

    lax.fori_loop(0, count, body, 0, unroll=4)


def pair_up(first, second, low):
    return jnp.where(low, first, pltpu.roll(second, 64, 1)), jnp.where(low, pltpu.roll(first, 64, 1), second)


def pack_kernel(place, amplitudes, *outs):
    for shift, out in enumerate(outs):
        piece = lax.rem(place[0] + shift, 4)
        lanes = pl.ds(pl.multiple_of(piece // 2 * 128, 128), 128)
        upper, lower = amplitudes[0, :, lanes].astype(F32), amplitudes[1, :, lanes].astype(F32)
        low = lax.broadcasted_iota(jnp.int32, upper.shape, 1) < 64
        left, right = pair_up(upper, lower, low)
        out[...] = jnp.where(lax.rem(piece, 2) == 0, left, right).astype(BF16)


def column_kernel(*refs):
    fields = refs[:CHUNKS]
    place, early, late, forward_lead, inverse_lead, forward_sub, inverse_sub = refs[CHUNKS : CHUNKS + 7]
    outs = refs[CHUNKS + 7 : 2 * CHUNKS + 7]
    loss, hold = refs[2 * CHUNKS + 7 :]
    count = SLAB // CHUNKS

    for chunk in range(CHUNKS):

        def forward(step, carry, chunk=chunk):
            y, r = step // count, lax.rem(step, count)
            at = y * SLAB + chunk * count + r
            low = lax.broadcasted_iota(jnp.int32, (8, 128), 1) < 64
            parts = [[[], []], [[], []]]
            for x in range(4):
                for core in range(2):
                    block = fields[chunk][(x * 4 + y) * 2 + core, r].astype(F32)
                    for pair in range(2):
                        real_part, imag_part = pair_up(block[pair * 16 : pair * 16 + 8], block[pair * 16 + 8 : pair * 16 + 16], low)
                        parts[0][pair].append(real_part)
                        parts[1][pair].append(imag_part)
            stacked = jnp.concatenate(
                [jnp.concatenate([jnp.concatenate(parts[part][pair], axis=0) for pair in range(2)], axis=1) for part in range(2)], axis=0
            ).astype(BF16)
            result = jnp.dot(forward_lead[at], stacked, preferred_element_type=F32)
            for part in range(2):
                for pair in range(2):
                    hold[part, pair, pl.ds(at, LEAD, stride=STRIDE), :] = result[part * 64 : part * 64 + 64, pair * 128 : pair * 128 + 128]
            return carry

        lax.fori_loop(0, 4 * count, forward, 0, unroll=8)

    loss[...] = jnp.zeros_like(loss)

    def middle(amplitudes, first_k1, index, carry):
        k1_low = first_k1 + index
        low = lax.broadcasted_iota(jnp.int32, (SUB, 128), 1) < 64
        measured = [[], []]
        for pair in range(2):
            first, second = (amplitudes[lax.rem(place[0] + 4 - b, 4), index].astype(F32) for b in (pair * 2, pair * 2 + 1))
            for high, values in enumerate(pair_up(first, second, low)):
                measured[high].append(values)
        places = [pl.ds(pl.multiple_of((k1_low + high * 32) * STRIDE, 8), SUB) for high in range(2)]
        stacked = [
            jnp.concatenate(
                [jnp.concatenate([hold[part, pair, at, :].astype(BF16) for pair in range(2)], axis=1) for part in range(2)], axis=0
            )
            for at in places
        ]
        spectra = [jnp.dot(forward_sub[...], values, preferred_element_type=F32) for values in stacked]
        weighted, total = [], 0.0
        for spectrum, values in zip(spectra, measured):
            real_part, imag_part = spectrum[:SUB] * (1.0 / N), spectrum[SUB:] * (1.0 / N)
            amplitude = jnp.concatenate(values, axis=1)
            squared = real_part * real_part + imag_part * imag_part + EPSILON
            inverse = lax.rsqrt(squared)
            kept = 1.0 - amplitude * inverse
            misfit = squared * inverse - amplitude
            total = total + jnp.sum((misfit * misfit).reshape(SUB // 8, 8, 256), axis=0)
            weighted.append(jnp.concatenate([(real_part * kept).astype(BF16), (imag_part * kept).astype(BF16)], axis=0))
        results = [jnp.dot(inverse_sub[...], values, preferred_element_type=F32) for values in weighted]
        loss[...] += total
        for at, result in zip(places, results):
            for part in range(2):
                for pair in range(2):
                    hold[part, pair, at, :] = result[part * SUB : part * SUB + SUB, pair * 128 : pair * 128 + 128]
        return carry

    lax.fori_loop(0, EARLY // SUB, functools.partial(middle, early, 0), 0, unroll=2)
    lax.fori_loop(0, 32 - EARLY // SUB, functools.partial(middle, late, EARLY // SUB), 0, unroll=2)

    for chunk in range(CHUNKS):

        def inverse(step, carry, chunk=chunk):
            y, r = step // count, lax.rem(step, count)
            at = y * SLAB + chunk * count + r
            low = lax.broadcasted_iota(jnp.int32, (8, 128), 1) < 64
            stacked = jnp.concatenate(
                [jnp.concatenate([hold[part, pair, pl.ds(at, LEAD, stride=STRIDE), :] for pair in range(2)], axis=1) for part in range(2)],
                axis=0,
            ).astype(BF16)
            result = jnp.dot(inverse_lead[at], stacked, preferred_element_type=F32)
            for x in range(4):
                for core in range(2):
                    row = (x * 2 + core) * 8
                    block = []
                    for pair in range(2):
                        real_part = result[row : row + 8, pair * 128 : pair * 128 + 128]
                        imag_part = result[64 + row : 64 + row + 8, pair * 128 : pair * 128 + 128]
                        block.extend(pair_up(real_part, imag_part, low))
                    outs[chunk][(x * 4 + y) * 2 + core, r] = jnp.concatenate(block, axis=0).astype(BF16)
            return carry

        lax.fori_loop(0, 4 * count, inverse, 0, unroll=8)


VMEM = pl.BlockSpec(memory_space=pltpu.VMEM)
SMEM = pl.BlockSpec(memory_space=pltpu.SMEM)


def params(mib):
    return pltpu.CompilerParams(vmem_limit_bytes=mib * 2**20)


def cost(flops, moved):
    return pl.CostEstimate(flops=flops, bytes_accessed=moved, transcendentals=0)


def row_forward(table, first_row, scalars, image):
    count = image.shape[2]
    return pl.pallas_call(
        functools.partial(row_forward_kernel, first_row),
        out_shape=jax.ShapeDtypeStruct((32, count, 32, 128), BF16),
        in_specs=[SMEM] + [VMEM] * 4,
        out_specs=VMEM,
        scratch_shapes=[pltpu.VMEM((2, 512, 128), F32)],
        compiler_params=params(40),
        cost_estimate=cost(count * 10**9, count * 2**19),
        name="row_forward",
    )(scalars, image, table["forward_row_lead"], table["forward_row_sub"], table["forward_turn"])


def row_inverse(table, first_row, scalars, field):
    count = field.shape[1]
    return pl.pallas_call(
        functools.partial(row_inverse_kernel, first_row),
        out_shape=jax.ShapeDtypeStruct((8, 2, count, LEAD, SUB), BF16),
        in_specs=[SMEM] + [VMEM] * 4,
        out_specs=VMEM,
        scratch_shapes=[pltpu.VMEM((2, 512, 128), F32)],
        compiler_params=params(40),
        cost_estimate=cost(count * 10**9, count * 2**19),
        name="row_inverse",
    )(scalars, field, table["inverse_row_lead"], table["inverse_row_sub"], table["inverse_turn"])


def pack(place, amplitudes):
    rows = N // 2
    step = 512
    return pl.pallas_call(
        pack_kernel,
        grid=(rows // step,),
        out_shape=[jax.ShapeDtypeStruct((rows, 128), BF16)] * 4,
        in_specs=[SMEM, pl.BlockSpec((2, step, 256), lambda i: (0, i, 0))],
        out_specs=[pl.BlockSpec((step, 128), lambda i: (i, 0))] * 4,
        cost_estimate=cost(10**7, 2**23),
        name="pack",
    )(place, amplitudes.reshape(2, rows, 256))


def columns(table, fields, place, amplitudes, forward_lead, inverse_lead):
    count = SLAB // CHUNKS
    result = pl.pallas_call(
        column_kernel,
        out_shape=[jax.ShapeDtypeStruct((32, count, 32, 128), BF16)] * CHUNKS + [jax.ShapeDtypeStruct((8, 256), F32)],
        in_specs=[VMEM] * CHUNKS + [SMEM] + [VMEM] * 6,
        out_specs=[VMEM] * (CHUNKS + 1),
        scratch_shapes=[pltpu.VMEM((2, 2, LEAD * STRIDE, 128), F32)],
        compiler_params=params(58),
        cost_estimate=cost(40 * 10**9, 2**25),
        name="columns",
    )(*fields, place, *amplitudes, forward_lead, inverse_lead, table["forward_sub"], table["inverse_sub"])
    return result[:-1], result[-1]


def shift_by(piece, axis, shift):
    return piece if shift == 0 else lax.ppermute(piece, axis, [(i, (i + shift) % 4) for i in range(4)])


def fold(value, axis, distance):
    return value + lax.ppermute(value, axis, [(i, i ^ distance) for i in range(lax.axis_size(axis))])


def shards(table, image_field, amplitudes, mask_ids):
    plane = ("x", "y", "core")
    x, zh, core, zl, y = (lax.axis_index(name) for name in ("x", "zh", "core", "zl", "y"))
    swap = [(a * 4 + b, b * 4 + a) for a in range(4) for b in range(4)]
    mask_term = (lax.ppermute(mask_ids, ("zh", "y"), swap) + 1) * jnp.int32(MASK_PRIME)
    zs = jnp.arange(8, dtype=jnp.int32)
    first_rows = (((x * 4 + zs // 2) * 2 + core) * 8 + zs % 2 * 4 + y) * SLAB
    scalars = jnp.concatenate([first_rows.astype(jnp.int32), mask_term])
    count = SLAB // CHUNKS

    image = image_field.reshape(2, SLAB, LEAD, SUB)
    slabs = [lax.all_gather(image[:, c * count : (c + 1) * count], ("zh", "zl"), axis=0) for c in range(CHUNKS)]

    packed = pack(y[None].astype(jnp.int32), amplitudes)
    spread = [shift_by(piece, "y", s) for s, piece in enumerate(packed)]
    spread, slabs[0] = lax.optimization_barrier((spread, slabs[0]))
    spread = jnp.stack(spread)
    sent = [row_forward(table, 0, scalars, slabs[0])]
    fields = [lax.all_to_all(sent[0], plane, 0, 0, tiled=True)]

    def to_planes(rows, first, last):
        cut = [lax.dynamic_slice_in_dim(rows[:, first:last], lax.rem(y - zh - t + 8, 4), 1, 0)[0] for t in range(4)]
        return [shift_by(piece, "zh", t) for t, piece in enumerate(cut)]

    early = to_planes(spread, 0, EARLY)
    spread, slabs[-1] = lax.optimization_barrier((spread, slabs[-1]))
    late = to_planes(spread, EARLY, N // 2)
    slabs[-1], fields[0], early = lax.optimization_barrier((slabs[-1], fields[0], early))
    packed = [jnp.stack(pieces).reshape(4, -1, SUB, 128) for pieces in (early, late)]
    forward_lead = column_tables(table, "forward")
    inverse_lead = column_tables(table, "inverse")
    sent.extend(row_forward(table, c * count, scalars, slabs[c]) for c in range(1, CHUNKS))
    fields.extend(lax.all_to_all(piece, plane, 0, 0, tiled=True) for piece in sent[1:])
    returned, loss = columns(table, fields, zh[None].astype(jnp.int32), packed, forward_lead, inverse_lead)
    loss_total = jnp.sum(loss).reshape(1)
    for axis, distance in (("zl", 1), ("zh", 1), ("zh", 2), ("core", 1)):
        loss_total = fold(loss_total, axis, distance)
    pieces = []
    returned = list(returned)
    for c in range(CHUNKS):
        back = lax.all_to_all(returned[c], plane, 0, 0, tiled=True)
        if c == 0:
            loss_total, back, returned[1:] = lax.optimization_barrier((loss_total, back, returned[1:]))
            for axis, distance in (("x", 1), ("x", 2), ("y", 1), ("y", 2)):
                loss_total = fold(loss_total, axis, distance)
        else:
            loss_total, back = lax.optimization_barrier((loss_total, back))
        term = row_inverse(table, c * count, scalars, back)
        pieces.append(lax.psum_scatter(term, ("zh", "zl"), scatter_dimension=0, tiled=False))
    gradient = jnp.concatenate(pieces, axis=1).astype(F32).reshape(2, SLAB, N)
    return gradient, loss_total[0] / (8 * N * N)


def solution(mesh):
    fine = Mesh(mesh.devices.reshape(4, 4, 2, 2, 4), ("x", "zh", "core", "zl", "y"))
    rows, mask = ("x", "zh", "core"), ("zl", "y")
    return jax.shard_map(
        functools.partial(shards, tables()),
        mesh=fine,
        in_specs=(P(None, rows + mask, None), P(mask, None, rows), P(mask)),
        out_specs=(P(None, rows + mask, None), P()),
        check_vma=False,
    )
```

```python
import functools
import math

import jax
import jax.numpy as jnp
import ml_dtypes
import numpy as np
from jax import lax
from jax.experimental import pallas as pl
from jax.experimental.pallas import tpu as pltpu
from jax.sharding import Mesh
from jax.sharding import PartitionSpec as P

N = 8192
LEAD = 64
SUB = 128
SLAB = 32
STRIDE = 136
EPSILON = 0.25
CHUNKS = 2
EARLY = 1280
ROW_PRIME, COLUMN_PRIME, MASK_PRIME, MIX_PRIME = 73856093, 19349663, 83492791, 1274126177
BF16 = jnp.bfloat16
F32 = jnp.float32


def rounded(values):
    return values.astype(ml_dtypes.bfloat16).astype(np.float32)


def unit_table(outputs, inputs, length, direction):
    angles = (outputs[:, None] * inputs[None, :] % length) * (2.0 * math.pi / length)
    return np.cos(angles), direction * np.sin(angles)


def block_form(real_part, imag_part):
    return np.block([[real_part, -imag_part], [imag_part, real_part]])


def orders():
    x, core, jh, b = np.meshgrid(np.arange(4), np.arange(2), np.arange(2), np.arange(4), indexing="ij")
    k1 = (x * 16 + b * 4 + core * 2 + jh).reshape(-1)
    x, core, zh, zl = np.meshgrid(np.arange(4), np.arange(2), np.arange(4), np.arange(2), indexing="ij")
    n1 = (x * 16 + zh * 4 + core * 2 + zl).reshape(-1)
    return k1, n1


def tables():
    k1_order, n1_order = orders()
    lead, sub = np.arange(LEAD), np.arange(SUB)
    out = {}
    lanes = np.arange(256)
    half, part, low = lanes // 128, (lanes // 64) % 2, lanes % 64
    split = part * 128 + half * 64 + low
    for name, direction in (("forward", -1.0), ("inverse", 1.0)):
        sub_full = block_form(*map(rounded, unit_table(sub, sub, SUB, direction)))
        out[name + "_sub"] = sub_full.astype(ml_dtypes.bfloat16)
        if name == "forward":
            row_lead = block_form(*map(rounded, unit_table(k1_order, lead, LEAD, direction)))
            row_sub = sub_full.T[:, split]
            turn = unit_table(k1_order, sub, N, direction)
            col = tuple(map(rounded, unit_table(lead, n1_order, LEAD, direction)))
        else:
            row_lead = block_form(*map(rounded, unit_table(lead, k1_order, LEAD, direction)))
            row_sub = sub_full.T[split, :]
            turn = tuple(np.repeat(t, 8, axis=0) for t in unit_table(k1_order, sub, N, direction))
            col = tuple(map(rounded, unit_table(n1_order, lead, LEAD, direction)))
        out[name + "_row_lead"] = row_lead.astype(ml_dtypes.bfloat16)
        out[name + "_row_sub"] = row_sub.astype(ml_dtypes.bfloat16)
        out[name + "_turn"] = np.stack(turn).astype(np.float32)
        col_plain = block_form(*col).astype(np.float32)
        col_quarter = block_form(-col[1], col[0]).astype(np.float32)
        out[name + "_col"] = np.stack([col_plain, col_quarter])
        twist = unit_table(sub, np.concatenate([lead, lead]), N, direction)
        out[name + "_col_turn"] = np.stack(twist).astype(np.float32)
    return out


def column_tables(table, name):
    plain, quarter = table[name + "_col"]
    cosine, sine = table[name + "_col_turn"]
    plain, quarter, cosine, sine = map(jnp.asarray, (plain, quarter, cosine, sine))
    if name == "forward":
        cosine, sine = cosine[:, :, None], sine[:, :, None]
    else:
        cosine, sine = cosine[:, None, :], sine[:, None, :]
    return (plain[None] * cosine + quarter[None] * sine).astype(BF16)


def phase_code(hashed_columns, row_term):
    mixed = hashed_columns ^ row_term
    mixed = mixed ^ lax.shift_right_logical(mixed, jnp.int32(13))
    mixed = mixed * jnp.int32(MIX_PRIME)
    mixed = mixed ^ lax.shift_right_logical(mixed, jnp.int32(16))
    return lax.shift_right_logical(mixed, jnp.int32(28))


def column_hash():
    shape = (LEAD, SUB)
    column = lax.broadcasted_iota(jnp.int32, shape, 0) * SUB + lax.broadcasted_iota(jnp.int32, shape, 1)
    return column * jnp.int32(COLUMN_PRIME)


def quarter_turn(real_part, imag_part, code, forward):
    odd = (code & 1) == 1
    first = jnp.where(odd, imag_part, real_part)
    second = jnp.where(odd, real_part, imag_part)
    high = (code & 2) == 2
    mixed = ((code ^ lax.shift_right_logical(code, jnp.int32(1))) & 1) == 1
    flip_real, flip_imag = (mixed, high) if forward else (high, mixed)
    return jnp.where(flip_real, -first, first), jnp.where(flip_imag, -second, second)


def row_forward_kernel(first_row, scalars, image, lead_table, sub_table, turn, out, swap):
    count = image.shape[2]
    columns = column_hash()

    def body(r, carry):
        stacked = []
        for zs in range(8):
            row = scalars[zs] + first_row + r
            code = phase_code(columns, (row * jnp.int32(ROW_PRIME)) ^ scalars[8])
            real_part, imag_part = image[zs, 0, r].astype(F32), image[zs, 1, r].astype(F32)
            real_part, imag_part = quarter_turn(real_part, imag_part, code, True)
            stacked.append(jnp.concatenate([real_part, imag_part], axis=0).astype(BF16))
        first = jnp.dot(lead_table[...], jnp.concatenate(stacked, axis=1), preferred_element_type=F32)
        cosine, sine = turn[0], turn[1]
        middle = []
        for zs in range(8):
            real_part, imag_part = first[:LEAD, zs * 128 : zs * 128 + 128], first[LEAD:, zs * 128 : zs * 128 + 128]
            turned = [real_part * cosine - imag_part * sine, real_part * sine + imag_part * cosine]
            middle.append(jnp.concatenate(turned, axis=1).astype(BF16))
        second = jnp.dot(jnp.concatenate(middle, axis=0), sub_table[...], preferred_element_type=F32)
        for zs in range(8):
            for half in range(2):
                swap[half, pl.ds(zs, LEAD, stride=8), :] = second[zs * LEAD : (zs + 1) * LEAD, half * 128 : half * 128 + 128]
        for x in range(4):
            for core in range(2):
                for jh in range(2):
                    at = ((x * 2 + core) * 2 + jh) * 32
                    for half in range(2):
                        out[(x * 4 + jh * 2 + half) * 2 + core, r] = swap[half, at : at + 32, :].astype(BF16)
        return carry

    lax.fori_loop(0, count, body, 0, unroll=4)


def row_inverse_kernel(first_row, scalars, field, lead_table, sub_table, turn, out, swap):
    count = field.shape[1]
    columns = column_hash()

    def body(r, carry):
        blocks = []
        for x in range(4):
            for core in range(2):
                for jh in range(2):
                    pair = [field[(x * 4 + jh * 2 + half) * 2 + core, r] for half in range(2)]
                    blocks.append(jnp.concatenate(pair, axis=1))
        first = jnp.dot(jnp.concatenate(blocks, axis=0), sub_table[...], preferred_element_type=F32)
        real_part, imag_part = first[:, :128], first[:, 128:]
        cosine, sine = turn[0], turn[1]
        swap[0] = real_part * cosine - imag_part * sine
        swap[1] = real_part * sine + imag_part * cosine
        middle = []
        for zs in range(8):
            parts = [swap[part, pl.ds(zs, LEAD, stride=8), :] for part in range(2)]
            middle.append(jnp.concatenate(parts, axis=0).astype(BF16))
        second = jnp.dot(lead_table[...], jnp.concatenate(middle, axis=1), preferred_element_type=F32)
        second = second * (1.0 / N)
        for zs in range(8):
            row = scalars[zs] + first_row + r
            code = phase_code(columns, (row * jnp.int32(ROW_PRIME)) ^ scalars[8])
            real_part, imag_part = second[:LEAD, zs * 128 : zs * 128 + 128], second[LEAD:, zs * 128 : zs * 128 + 128]
            real_part, imag_part = quarter_turn(real_part, imag_part, code, False)
            out[zs, 0, r] = real_part.astype(BF16)
            out[zs, 1, r] = imag_part.astype(BF16)
        return carry

    lax.fori_loop(0, count, body, 0, unroll=4)


def pair_up(first, second, low):
    return jnp.where(low, first, pltpu.roll(second, 64, 1)), jnp.where(low, pltpu.roll(first, 64, 1), second)


def pack_kernel(place, amplitudes, *outs):
    for shift, out in enumerate(outs):
        piece = lax.rem(place[0] + shift, 4)
        lanes = pl.ds(pl.multiple_of(piece // 2 * 128, 128), 128)
        upper, lower = amplitudes[0, :, lanes].astype(F32), amplitudes[1, :, lanes].astype(F32)
        low = lax.broadcasted_iota(jnp.int32, upper.shape, 1) < 64
        left, right = pair_up(upper, lower, low)
        out[...] = jnp.where(lax.rem(piece, 2) == 0, left, right).astype(BF16)


def column_kernel(*refs):
    fields = refs[:CHUNKS]
    place, early, late, forward_lead, inverse_lead, forward_sub, inverse_sub = refs[CHUNKS : CHUNKS + 7]
    outs = refs[CHUNKS + 7 : 2 * CHUNKS + 7]
    loss, hold = refs[2 * CHUNKS + 7 :]
    count = SLAB // CHUNKS

    for chunk in range(CHUNKS):

        def forward(step, carry, chunk=chunk):
            y, r = step // count, lax.rem(step, count)
            at = y * SLAB + chunk * count + r
            low = lax.broadcasted_iota(jnp.int32, (8, 128), 1) < 64
            parts = [[[], []], [[], []]]
            for x in range(4):
                for core in range(2):
                    block = fields[chunk][(x * 4 + y) * 2 + core, r].astype(F32)
                    for pair in range(2):
                        real_part, imag_part = pair_up(block[pair * 16 : pair * 16 + 8], block[pair * 16 + 8 : pair * 16 + 16], low)
                        parts[0][pair].append(real_part)
                        parts[1][pair].append(imag_part)
            stacked = jnp.concatenate(
                [jnp.concatenate([jnp.concatenate(parts[part][pair], axis=0) for pair in range(2)], axis=1) for part in range(2)], axis=0
            ).astype(BF16)
            result = jnp.dot(forward_lead[at], stacked, preferred_element_type=F32)
            for part in range(2):
                for pair in range(2):
                    hold[part, pair, pl.ds(at, LEAD, stride=STRIDE), :] = result[part * 64 : part * 64 + 64, pair * 128 : pair * 128 + 128]
            return carry

        lax.fori_loop(0, 4 * count, forward, 0, unroll=8)

    loss[...] = jnp.zeros_like(loss)

    def middle(amplitudes, first_k1, index, carry):
        k1_low = first_k1 + index
        low = lax.broadcasted_iota(jnp.int32, (SUB, 128), 1) < 64
        measured = [[], []]
        for pair in range(2):
            first, second = (amplitudes[lax.rem(place[0] + 4 - b, 4), index].astype(F32) for b in (pair * 2, pair * 2 + 1))
            for high, values in enumerate(pair_up(first, second, low)):
                measured[high].append(values)
        places = [pl.ds(pl.multiple_of((k1_low + high * 32) * STRIDE, 8), SUB) for high in range(2)]
        stacked = [
            jnp.concatenate(
                [jnp.concatenate([hold[part, pair, at, :].astype(BF16) for pair in range(2)], axis=1) for part in range(2)], axis=0
            )
            for at in places
        ]
        spectra = [jnp.dot(forward_sub[...], values, preferred_element_type=F32) for values in stacked]
        weighted, total = [], 0.0
        for spectrum, values in zip(spectra, measured):
            real_part, imag_part = spectrum[:SUB] * (1.0 / N), spectrum[SUB:] * (1.0 / N)
            amplitude = jnp.concatenate(values, axis=1)
            squared = real_part * real_part + imag_part * imag_part + EPSILON
            inverse = lax.rsqrt(squared)
            kept = 1.0 - amplitude * inverse
            misfit = squared * inverse - amplitude
            total = total + jnp.sum((misfit * misfit).reshape(SUB // 8, 8, 256), axis=0)
            weighted.append(jnp.concatenate([(real_part * kept).astype(BF16), (imag_part * kept).astype(BF16)], axis=0))
        results = [jnp.dot(inverse_sub[...], values, preferred_element_type=F32) for values in weighted]
        loss[...] += total
        for at, result in zip(places, results):
            for part in range(2):
                for pair in range(2):
                    hold[part, pair, at, :] = result[part * SUB : part * SUB + SUB, pair * 128 : pair * 128 + 128]
        return carry

    lax.fori_loop(0, EARLY // SUB, functools.partial(middle, early, 0), 0, unroll=2)
    lax.fori_loop(0, 32 - EARLY // SUB, functools.partial(middle, late, EARLY // SUB), 0, unroll=2)

    for chunk in range(CHUNKS):

        def inverse(step, carry, chunk=chunk):
            y, r = step // count, lax.rem(step, count)
            at = y * SLAB + chunk * count + r
            low = lax.broadcasted_iota(jnp.int32, (8, 128), 1) < 64
            stacked = jnp.concatenate(
                [jnp.concatenate([hold[part, pair, pl.ds(at, LEAD, stride=STRIDE), :] for pair in range(2)], axis=1) for part in range(2)],
                axis=0,
            ).astype(BF16)
            result = jnp.dot(inverse_lead[at], stacked, preferred_element_type=F32)
            for x in range(4):
                for core in range(2):
                    row = (x * 2 + core) * 8
                    block = []
                    for pair in range(2):
                        real_part = result[row : row + 8, pair * 128 : pair * 128 + 128]
                        imag_part = result[64 + row : 64 + row + 8, pair * 128 : pair * 128 + 128]
                        block.extend(pair_up(real_part, imag_part, low))
                    outs[chunk][(x * 4 + y) * 2 + core, r] = jnp.concatenate(block, axis=0).astype(BF16)
            return carry

        lax.fori_loop(0, 4 * count, inverse, 0, unroll=8)


VMEM = pl.BlockSpec(memory_space=pltpu.VMEM)
SMEM = pl.BlockSpec(memory_space=pltpu.SMEM)


def params(mib):
    return pltpu.CompilerParams(vmem_limit_bytes=mib * 2**20)


def cost(flops, moved):
    return pl.CostEstimate(flops=flops, bytes_accessed=moved, transcendentals=0)


def row_forward(table, first_row, scalars, image):
    count = image.shape[2]
    return pl.pallas_call(
        functools.partial(row_forward_kernel, first_row),
        out_shape=jax.ShapeDtypeStruct((32, count, 32, 128), BF16),
        in_specs=[SMEM] + [VMEM] * 4,
        out_specs=VMEM,
        scratch_shapes=[pltpu.VMEM((2, 512, 128), F32)],
        compiler_params=params(40),
        cost_estimate=cost(count * 10**9, count * 2**19),
        name="row_forward",
    )(scalars, image, table["forward_row_lead"], table["forward_row_sub"], table["forward_turn"])


def row_inverse(table, first_row, scalars, field):
    count = field.shape[1]
    return pl.pallas_call(
        functools.partial(row_inverse_kernel, first_row),
        out_shape=jax.ShapeDtypeStruct((8, 2, count, LEAD, SUB), BF16),
        in_specs=[SMEM] + [VMEM] * 4,
        out_specs=VMEM,
        scratch_shapes=[pltpu.VMEM((2, 512, 128), F32)],
        compiler_params=params(40),
        cost_estimate=cost(count * 10**9, count * 2**19),
        name="row_inverse",
    )(scalars, field, table["inverse_row_lead"], table["inverse_row_sub"], table["inverse_turn"])


def pack(place, amplitudes):
    rows = N // 2
    step = 512
    return pl.pallas_call(
        pack_kernel,
        grid=(rows // step,),
        out_shape=[jax.ShapeDtypeStruct((rows, 128), BF16)] * 4,
        in_specs=[SMEM, pl.BlockSpec((2, step, 256), lambda i: (0, i, 0))],
        out_specs=[pl.BlockSpec((step, 128), lambda i: (i, 0))] * 4,
        cost_estimate=cost(10**7, 2**23),
        name="pack",
    )(place, amplitudes.reshape(2, rows, 256))


def columns(table, fields, place, amplitudes, forward_lead, inverse_lead):
    count = SLAB // CHUNKS
    result = pl.pallas_call(
        column_kernel,
        out_shape=[jax.ShapeDtypeStruct((32, count, 32, 128), BF16)] * CHUNKS + [jax.ShapeDtypeStruct((8, 256), F32)],
        in_specs=[VMEM] * CHUNKS + [SMEM] + [VMEM] * 6,
        out_specs=[VMEM] * (CHUNKS + 1),
        scratch_shapes=[pltpu.VMEM((2, 2, LEAD * STRIDE, 128), F32)],
        compiler_params=params(58),
        cost_estimate=cost(40 * 10**9, 2**25),
        name="columns",
    )(*fields, place, *amplitudes, forward_lead, inverse_lead, table["forward_sub"], table["inverse_sub"])
    return result[:-1], result[-1]


def shift_by(piece, axis, shift):
    return piece if shift == 0 else lax.ppermute(piece, axis, [(i, (i + shift) % 4) for i in range(4)])


def fold(value, axis, distance):
    return value + lax.ppermute(value, axis, [(i, i ^ distance) for i in range(lax.axis_size(axis))])


def shards(table, image_field, amplitudes, mask_ids):
    plane = ("x", "y", "core")
    x, zh, core, zl, y = (lax.axis_index(name) for name in ("x", "zh", "core", "zl", "y"))
    swap = [(a * 4 + b, b * 4 + a) for a in range(4) for b in range(4)]
    mask_term = (lax.ppermute(mask_ids, ("zh", "y"), swap) + 1) * jnp.int32(MASK_PRIME)
    zs = jnp.arange(8, dtype=jnp.int32)
    first_rows = (((x * 4 + zs // 2) * 2 + core) * 8 + zs % 2 * 4 + y) * SLAB
    scalars = jnp.concatenate([first_rows.astype(jnp.int32), mask_term])
    count = SLAB // CHUNKS

    image = image_field.reshape(2, SLAB, LEAD, SUB)
    slabs = [lax.all_gather(image[:, c * count : (c + 1) * count], ("zh", "zl"), axis=0) for c in range(CHUNKS)]

    packed = pack(y[None].astype(jnp.int32), amplitudes)
    spread = [shift_by(piece, "y", s) for s, piece in enumerate(packed)]
    spread, slabs[0] = lax.optimization_barrier((spread, slabs[0]))
    spread = jnp.stack(spread)
    sent = [row_forward(table, 0, scalars, slabs[0])]
    fields = [lax.all_to_all(sent[0], plane, 0, 0, tiled=True)]

    def to_planes(rows, first, last):
        cut = [lax.dynamic_slice_in_dim(rows[:, first:last], lax.rem(y - zh - t + 8, 4), 1, 0)[0] for t in range(4)]
        return [shift_by(piece, "zh", t) for t, piece in enumerate(cut)]

    early = to_planes(spread, 0, EARLY)
    spread, slabs[-1] = lax.optimization_barrier((spread, slabs[-1]))
    late = to_planes(spread, EARLY, N // 2)
    slabs[-1], fields[0], early = lax.optimization_barrier((slabs[-1], fields[0], early))
    packed = [jnp.stack(pieces).reshape(4, -1, SUB, 128) for pieces in (early, late)]
    forward_lead = column_tables(table, "forward")
    inverse_lead = column_tables(table, "inverse")
    sent.extend(row_forward(table, c * count, scalars, slabs[c]) for c in range(1, CHUNKS))
    fields.extend(lax.all_to_all(piece, plane, 0, 0, tiled=True) for piece in sent[1:])
    returned, loss = columns(table, fields, zh[None].astype(jnp.int32), packed, forward_lead, inverse_lead)
    loss_total = jnp.sum(loss).reshape(1)
    for axis, distance in (("zl", 1), ("zh", 1), ("zh", 2)):
        loss_total = fold(loss_total, axis, distance)
    pieces = []
    returned = list(returned)
    for c in range(CHUNKS):
        back = lax.all_to_all(returned[c], plane, 0, 0, tiled=True)
        if c == 0:
            loss_total, back, returned[1:] = lax.optimization_barrier((loss_total, back, returned[1:]))
            loss_total = fold(loss_total, "core", 1)
            loss_total, back = lax.optimization_barrier((loss_total, back))
        term = row_inverse(table, c * count, scalars, back)
        if c == CHUNKS - 1:
            loss_total, term = lax.optimization_barrier((loss_total, term))
        pieces.append(lax.psum_scatter(term, ("zh", "zl"), scatter_dimension=0, tiled=False))
    for axis, distance in (("x", 1), ("x", 2), ("y", 1), ("y", 2)):
        loss_total = fold(loss_total, axis, distance)
    gradient = jnp.concatenate(pieces, axis=1).astype(F32).reshape(2, SLAB, N)
    return gradient, loss_total[0] / (8 * N * N)


def solution(mesh):
    fine = Mesh(mesh.devices.reshape(4, 4, 2, 2, 4), ("x", "zh", "core", "zl", "y"))
    rows, mask = ("x", "zh", "core"), ("zl", "y")
    return jax.shard_map(
        functools.partial(shards, tables()),
        mesh=fine,
        in_specs=(P(None, rows + mask, None), P(mask, None, rows), P(mask)),
        out_specs=(P(None, rows + mask, None), P()),
        check_vma=False,
    )
```

```python
import functools
import math

import jax
import jax.numpy as jnp
import ml_dtypes
import numpy as np
from jax import lax
from jax.experimental import pallas as pl
from jax.experimental.pallas import tpu as pltpu
from jax.sharding import Mesh
from jax.sharding import PartitionSpec as P

N = 8192
LEAD = 64
SUB = 128
SLAB = 32
STRIDE = 136
EPSILON = 0.25
CHUNKS = 2
EARLY = 1280
BLOCK = 4
ROW_PRIME, COLUMN_PRIME, MASK_PRIME, MIX_PRIME = 73856093, 19349663, 83492791, 1274126177
BF16 = jnp.bfloat16
F32 = jnp.float32


def rounded(values):
    return values.astype(ml_dtypes.bfloat16).astype(np.float32)


def unit_table(outputs, inputs, length, direction):
    angles = (outputs[:, None] * inputs[None, :] % length) * (2.0 * math.pi / length)
    return np.cos(angles), direction * np.sin(angles)


def block_form(real_part, imag_part):
    return np.block([[real_part, -imag_part], [imag_part, real_part]])


def orders():
    x, core, jh, b = np.meshgrid(np.arange(4), np.arange(2), np.arange(2), np.arange(4), indexing="ij")
    k1 = (x * 16 + b * 4 + core * 2 + jh).reshape(-1)
    x, core, zh, zl = np.meshgrid(np.arange(4), np.arange(2), np.arange(4), np.arange(2), indexing="ij")
    n1 = (x * 16 + zh * 4 + core * 2 + zl).reshape(-1)
    return k1, n1


def tables():
    k1_order, n1_order = orders()
    lead, sub = np.arange(LEAD), np.arange(SUB)
    out = {}
    lanes = np.arange(256)
    half, part, low = lanes // 128, (lanes // 64) % 2, lanes % 64
    split = part * 128 + half * 64 + low
    for name, direction in (("forward", -1.0), ("inverse", 1.0)):
        sub_full = block_form(*map(rounded, unit_table(sub, sub, SUB, direction)))
        out[name + "_sub"] = sub_full.astype(ml_dtypes.bfloat16)
        if name == "forward":
            row_lead = block_form(*map(rounded, unit_table(k1_order, lead, LEAD, direction)))
            row_sub = sub_full.T[:, split]
            turn = unit_table(k1_order, sub, N, direction)
            col = tuple(map(rounded, unit_table(lead, n1_order, LEAD, direction)))
        else:
            row_lead = block_form(*map(rounded, unit_table(lead, k1_order, LEAD, direction)))
            row_sub = sub_full.T[split, :]
            turn = tuple(np.repeat(t, 8, axis=0) for t in unit_table(k1_order, sub, N, direction))
            col = tuple(map(rounded, unit_table(n1_order, lead, LEAD, direction)))
        out[name + "_row_lead"] = row_lead.astype(ml_dtypes.bfloat16)
        out[name + "_row_sub"] = row_sub.astype(ml_dtypes.bfloat16)
        out[name + "_turn"] = np.stack(turn).astype(np.float32)
        col_plain = block_form(*col).astype(np.float32)
        col_quarter = block_form(-col[1], col[0]).astype(np.float32)
        out[name + "_col"] = np.stack([col_plain, col_quarter])
        twist = unit_table(sub, np.concatenate([lead, lead]), N, direction)
        out[name + "_col_turn"] = np.stack(twist).astype(np.float32)
    return out


def column_tables(table, name):
    plain, quarter = table[name + "_col"]
    cosine, sine = table[name + "_col_turn"]
    plain, quarter, cosine, sine = map(jnp.asarray, (plain, quarter, cosine, sine))
    if name == "forward":
        cosine, sine = cosine[:, :, None], sine[:, :, None]
    else:
        cosine, sine = cosine[:, None, :], sine[:, None, :]
    return (plain[None] * cosine + quarter[None] * sine).astype(BF16)


def phase_code(hashed_columns, row_term):
    mixed = hashed_columns ^ row_term
    mixed = mixed ^ lax.shift_right_logical(mixed, jnp.int32(13))
    mixed = mixed * jnp.int32(MIX_PRIME)
    mixed = mixed ^ lax.shift_right_logical(mixed, jnp.int32(16))
    return lax.shift_right_logical(mixed, jnp.int32(28))


def column_hash():
    shape = (LEAD, SUB)
    column = lax.broadcasted_iota(jnp.int32, shape, 0) * SUB + lax.broadcasted_iota(jnp.int32, shape, 1)
    return column * jnp.int32(COLUMN_PRIME)


def quarter_turn(real_part, imag_part, code, forward):
    odd = (code & 1) == 1
    first = jnp.where(odd, imag_part, real_part)
    second = jnp.where(odd, real_part, imag_part)
    high = (code & 2) == 2
    mixed = ((code ^ lax.shift_right_logical(code, jnp.int32(1))) & 1) == 1
    flip_real, flip_imag = (mixed, high) if forward else (high, mixed)
    return jnp.where(flip_real, -first, first), jnp.where(flip_imag, -second, second)


def row_forward_kernel(first_row, scalars, image, lead_table, sub_table, turn, out, swap):
    columns = column_hash()
    block_row = first_row + pl.program_id(0) * BLOCK

    def body(r, carry):
        stacked = []
        for zs in range(8):
            row = scalars[zs] + block_row + r
            code = phase_code(columns, (row * jnp.int32(ROW_PRIME)) ^ scalars[8])
            real_part, imag_part = image[zs, 0, r].astype(F32), image[zs, 1, r].astype(F32)
            real_part, imag_part = quarter_turn(real_part, imag_part, code, True)
            stacked.append(jnp.concatenate([real_part, imag_part], axis=0).astype(BF16))
        first = jnp.dot(lead_table[...], jnp.concatenate(stacked, axis=1), preferred_element_type=F32)
        cosine, sine = turn[0], turn[1]
        middle = []
        for zs in range(8):
            real_part, imag_part = first[:LEAD, zs * 128 : zs * 128 + 128], first[LEAD:, zs * 128 : zs * 128 + 128]
            turned = [real_part * cosine - imag_part * sine, real_part * sine + imag_part * cosine]
            middle.append(jnp.concatenate(turned, axis=1).astype(BF16))
        second = jnp.dot(jnp.concatenate(middle, axis=0), sub_table[...], preferred_element_type=F32)
        for zs in range(8):
            for half in range(2):
                swap[half, pl.ds(zs, LEAD, stride=8), :] = second[zs * LEAD : (zs + 1) * LEAD, half * 128 : half * 128 + 128]
        for x in range(4):
            for core in range(2):
                for jh in range(2):
                    at = ((x * 2 + core) * 2 + jh) * 32
                    for half in range(2):
                        out[(x * 4 + jh * 2 + half) * 2 + core, r] = swap[half, at : at + 32, :].astype(BF16)
        return carry

    lax.fori_loop(0, BLOCK, body, 0, unroll=True)


def row_inverse_kernel(first_row, scalars, field, lead_table, sub_table, turn, out, swap):
    columns = column_hash()
    block_row = first_row + pl.program_id(0) * BLOCK

    def body(r, carry):
        blocks = []
        for x in range(4):
            for core in range(2):
                for jh in range(2):
                    pair = [field[(x * 4 + jh * 2 + half) * 2 + core, r] for half in range(2)]
                    blocks.append(jnp.concatenate(pair, axis=1))
        first = jnp.dot(jnp.concatenate(blocks, axis=0), sub_table[...], preferred_element_type=F32)
        real_part, imag_part = first[:, :128], first[:, 128:]
        cosine, sine = turn[0], turn[1]
        swap[0] = real_part * cosine - imag_part * sine
        swap[1] = real_part * sine + imag_part * cosine
        middle = []
        for zs in range(8):
            parts = [swap[part, pl.ds(zs, LEAD, stride=8), :] for part in range(2)]
            middle.append(jnp.concatenate(parts, axis=0).astype(BF16))
        second = jnp.dot(lead_table[...], jnp.concatenate(middle, axis=1), preferred_element_type=F32)
        second = second * (1.0 / N)
        for zs in range(8):
            row = scalars[zs] + block_row + r
            code = phase_code(columns, (row * jnp.int32(ROW_PRIME)) ^ scalars[8])
            real_part, imag_part = second[:LEAD, zs * 128 : zs * 128 + 128], second[LEAD:, zs * 128 : zs * 128 + 128]
            real_part, imag_part = quarter_turn(real_part, imag_part, code, False)
            out[zs, 0, r] = real_part.astype(BF16)
            out[zs, 1, r] = imag_part.astype(BF16)
        return carry

    lax.fori_loop(0, BLOCK, body, 0, unroll=True)


def pair_up(first, second, low):
    return jnp.where(low, first, pltpu.roll(second, 64, 1)), jnp.where(low, pltpu.roll(first, 64, 1), second)


def pack_kernel(place, amplitudes, *outs):
    for shift, out in enumerate(outs):
        piece = lax.rem(place[0] + shift, 4)
        lanes = pl.ds(pl.multiple_of(piece // 2 * 128, 128), 128)
        upper, lower = amplitudes[0, :, lanes].astype(F32), amplitudes[1, :, lanes].astype(F32)
        low = lax.broadcasted_iota(jnp.int32, upper.shape, 1) < 64
        left, right = pair_up(upper, lower, low)
        out[...] = jnp.where(lax.rem(piece, 2) == 0, left, right).astype(BF16)


def column_kernel(*refs):
    fields = refs[:CHUNKS]
    place, early, late, forward_lead, inverse_lead, forward_sub, inverse_sub = refs[CHUNKS : CHUNKS + 7]
    outs = refs[CHUNKS + 7 : 2 * CHUNKS + 7]
    loss, hold = refs[2 * CHUNKS + 7 : 2 * CHUNKS + 9]
    buffers, sems = refs[2 * CHUNKS + 9 : -1], refs[-1]
    count = SLAB // CHUNKS

    operands = list(fields) + [forward_lead, early, late, inverse_lead]
    order = [0, CHUNKS] + list(range(1, CHUNKS)) + list(range(CHUNKS + 1, CHUNKS + 4))
    loads = [pltpu.make_async_copy(operand, buffers[n], sems.at[n]) for n, operand in enumerate(operands)]
    for n in order:
        loads[n].start()
    fields = buffers[:CHUNKS]
    forward_lead, early, late, inverse_lead = buffers[CHUNKS : CHUNKS + 4]
    stores = [pltpu.make_async_copy(buffers[CHUNKS + 4 + n], outs[n], sems.at[CHUNKS + 4 + n]) for n in range(CHUNKS)]
    outs = buffers[CHUNKS + 4 :]
    loads[CHUNKS].wait()

    for chunk in range(CHUNKS):
        loads[chunk].wait()

        def forward(step, carry, chunk=chunk):
            y, r = step // count, lax.rem(step, count)
            at = y * SLAB + chunk * count + r
            low = lax.broadcasted_iota(jnp.int32, (8, 128), 1) < 64
            parts = [[[], []], [[], []]]
            for x in range(4):
                for core in range(2):
                    block = fields[chunk][(x * 4 + y) * 2 + core, r].astype(F32)
                    for pair in range(2):
                        real_part, imag_part = pair_up(block[pair * 16 : pair * 16 + 8], block[pair * 16 + 8 : pair * 16 + 16], low)
                        parts[0][pair].append(real_part)
                        parts[1][pair].append(imag_part)
            stacked = jnp.concatenate(
                [jnp.concatenate([jnp.concatenate(parts[part][pair], axis=0) for pair in range(2)], axis=1) for part in range(2)], axis=0
            ).astype(BF16)
            result = jnp.dot(forward_lead[at], stacked, preferred_element_type=F32)
            for part in range(2):
                for pair in range(2):
                    hold[part, pair, pl.ds(at, LEAD, stride=STRIDE), :] = result[part * 64 : part * 64 + 64, pair * 128 : pair * 128 + 128]
            return carry

        lax.fori_loop(0, 4 * count, forward, 0, unroll=8)

    loss[...] = jnp.zeros_like(loss)
    for n in range(CHUNKS + 1, CHUNKS + 3):
        loads[n].wait()

    def middle(amplitudes, first_k1, index, carry):
        k1_low = first_k1 + index
        low = lax.broadcasted_iota(jnp.int32, (SUB, 128), 1) < 64
        measured = [[], []]
        for pair in range(2):
            first, second = (amplitudes[lax.rem(place[0] + 4 - b, 4), index].astype(F32) for b in (pair * 2, pair * 2 + 1))
            for high, values in enumerate(pair_up(first, second, low)):
                measured[high].append(values)
        places = [pl.ds(pl.multiple_of((k1_low + high * 32) * STRIDE, 8), SUB) for high in range(2)]
        stacked = [
            jnp.concatenate(
                [jnp.concatenate([hold[part, pair, at, :].astype(BF16) for pair in range(2)], axis=1) for part in range(2)], axis=0
            )
            for at in places
        ]
        spectra = [jnp.dot(forward_sub[...], values, preferred_element_type=F32) for values in stacked]
        weighted, total = [], 0.0
        for spectrum, values in zip(spectra, measured):
            real_part, imag_part = spectrum[:SUB] * (1.0 / N), spectrum[SUB:] * (1.0 / N)
            amplitude = jnp.concatenate(values, axis=1)
            squared = real_part * real_part + imag_part * imag_part + EPSILON
            inverse = lax.rsqrt(squared)
            kept = 1.0 - amplitude * inverse
            misfit = squared * inverse - amplitude
            total = total + jnp.sum((misfit * misfit).reshape(SUB // 8, 8, 256), axis=0)
            weighted.append(jnp.concatenate([(real_part * kept).astype(BF16), (imag_part * kept).astype(BF16)], axis=0))
        results = [jnp.dot(inverse_sub[...], values, preferred_element_type=F32) for values in weighted]
        loss[...] += total
        for at, result in zip(places, results):
            for part in range(2):
                for pair in range(2):
                    hold[part, pair, at, :] = result[part * SUB : part * SUB + SUB, pair * 128 : pair * 128 + 128]
        return carry

    lax.fori_loop(0, EARLY // SUB, functools.partial(middle, early, 0), 0, unroll=2)
    lax.fori_loop(0, 32 - EARLY // SUB, functools.partial(middle, late, EARLY // SUB), 0, unroll=2)

    loads[CHUNKS + 3].wait()
    for chunk in range(CHUNKS):

        def inverse(step, carry, chunk=chunk):
            y, r = step // count, lax.rem(step, count)
            at = y * SLAB + chunk * count + r
            low = lax.broadcasted_iota(jnp.int32, (8, 128), 1) < 64
            stacked = jnp.concatenate(
                [jnp.concatenate([hold[part, pair, pl.ds(at, LEAD, stride=STRIDE), :] for pair in range(2)], axis=1) for part in range(2)],
                axis=0,
            ).astype(BF16)
            result = jnp.dot(inverse_lead[at], stacked, preferred_element_type=F32)
            for x in range(4):
                for core in range(2):
                    row = (x * 2 + core) * 8
                    block = []
                    for pair in range(2):
                        real_part = result[row : row + 8, pair * 128 : pair * 128 + 128]
                        imag_part = result[64 + row : 64 + row + 8, pair * 128 : pair * 128 + 128]
                        block.extend(pair_up(real_part, imag_part, low))
                    outs[chunk][(x * 4 + y) * 2 + core, r] = jnp.concatenate(block, axis=0).astype(BF16)
            return carry

        lax.fori_loop(0, 4 * count, inverse, 0, unroll=8)
        stores[chunk].start()

    for store in stores:
        store.wait()


VMEM = pl.BlockSpec(memory_space=pltpu.VMEM)
ANY = pl.BlockSpec(memory_space=pl.ANY)
SMEM = pl.BlockSpec(memory_space=pltpu.SMEM)


def params(mib):
    return pltpu.CompilerParams(vmem_limit_bytes=mib * 2**20)


def cost(flops, moved):
    return pl.CostEstimate(flops=flops, bytes_accessed=moved, transcendentals=0)


def whole(array):
    return pl.BlockSpec(array.shape, lambda i: (0,) * array.ndim, pipeline_mode=pl.Buffered(1))


def row_forward(table, first_row, scalars, image):
    count = image.shape[2]
    constants = [table["forward_row_lead"], table["forward_row_sub"], table["forward_turn"]]
    return pl.pallas_call(
        functools.partial(row_forward_kernel, first_row),
        grid=(count // BLOCK,),
        out_shape=jax.ShapeDtypeStruct((32, count, 32, 128), BF16),
        in_specs=[SMEM, pl.BlockSpec((8, 2, BLOCK, LEAD, SUB), lambda i: (0, 0, i, 0, 0))] + [whole(c) for c in constants],
        out_specs=pl.BlockSpec((32, BLOCK, 32, 128), lambda i: (0, i, 0, 0)),
        scratch_shapes=[pltpu.VMEM((2, 512, 128), F32)],
        compiler_params=params(58),
        cost_estimate=cost(count * 10**9, count * 2**19),
        name="row_forward",
    )(scalars, image, *constants)


def row_inverse(table, first_row, scalars, field):
    count = field.shape[1]
    constants = [table["inverse_row_lead"], table["inverse_row_sub"], table["inverse_turn"]]
    return pl.pallas_call(
        functools.partial(row_inverse_kernel, first_row),
        grid=(count // BLOCK,),
        out_shape=jax.ShapeDtypeStruct((8, 2, count, LEAD, SUB), BF16),
        in_specs=[SMEM, pl.BlockSpec((32, BLOCK, 32, 128), lambda i: (0, i, 0, 0))] + [whole(c) for c in constants],
        out_specs=pl.BlockSpec((8, 2, BLOCK, LEAD, SUB), lambda i: (0, 0, i, 0, 0)),
        scratch_shapes=[pltpu.VMEM((2, 512, 128), F32)],
        compiler_params=params(58),
        cost_estimate=cost(count * 10**9, count * 2**19),
        name="row_inverse",
    )(scalars, field, *constants)


def pack(place, amplitudes):
    rows = N // 2
    step = 512
    return pl.pallas_call(
        pack_kernel,
        grid=(rows // step,),
        out_shape=[jax.ShapeDtypeStruct((rows, 128), BF16)] * 4,
        in_specs=[SMEM, pl.BlockSpec((2, step, 256), lambda i: (0, i, 0))],
        out_specs=[pl.BlockSpec((step, 128), lambda i: (i, 0))] * 4,
        cost_estimate=cost(10**7, 2**23),
        name="pack",
    )(place, amplitudes.reshape(2, rows, 256))


def columns(table, fields, place, amplitudes, forward_lead, inverse_lead):
    count = SLAB // CHUNKS
    moved = list(fields) + [forward_lead, *amplitudes, inverse_lead]
    out = jax.ShapeDtypeStruct((32, count, 32, 128), BF16)
    result = pl.pallas_call(
        column_kernel,
        out_shape=[out] * CHUNKS + [jax.ShapeDtypeStruct((8, 256), F32)],
        in_specs=[ANY] * CHUNKS + [SMEM] + [ANY] * 4 + [VMEM] * 2,
        out_specs=[ANY] * CHUNKS + [VMEM],
        scratch_shapes=[pltpu.VMEM((2, 2, LEAD * STRIDE, 128), F32)]
        + [pltpu.VMEM(array.shape, BF16) for array in moved + [out] * CHUNKS]
        + [pltpu.SemaphoreType.DMA((2 * CHUNKS + 4,))],
        compiler_params=params(58),
        cost_estimate=cost(40 * 10**9, 2**25),
        name="columns",
    )(*fields, place, *amplitudes, forward_lead, inverse_lead, table["forward_sub"], table["inverse_sub"])
    return result[:-1], result[-1]


def shift_by(piece, axis, shift):
    return piece if shift == 0 else lax.ppermute(piece, axis, [(i, (i + shift) % 4) for i in range(4)])


def fold(value, axis, distance):
    return value + lax.ppermute(value, axis, [(i, i ^ distance) for i in range(lax.axis_size(axis))])


def shards(table, image_field, amplitudes, mask_ids):
    plane = ("x", "y", "core")
    x, zh, core, zl, y = (lax.axis_index(name) for name in ("x", "zh", "core", "zl", "y"))
    swap = [(a * 4 + b, b * 4 + a) for a in range(4) for b in range(4)]
    mask_term = (lax.ppermute(mask_ids, ("zh", "y"), swap) + 1) * jnp.int32(MASK_PRIME)
    zs = jnp.arange(8, dtype=jnp.int32)
    first_rows = (((x * 4 + zs // 2) * 2 + core) * 8 + zs % 2 * 4 + y) * SLAB
    scalars = jnp.concatenate([first_rows.astype(jnp.int32), mask_term])
    count = SLAB // CHUNKS

    image = image_field.reshape(2, SLAB, LEAD, SUB)
    slabs = [lax.all_gather(image[:, c * count : (c + 1) * count], ("zh", "zl"), axis=0) for c in range(CHUNKS)]

    packed = pack(y[None].astype(jnp.int32), amplitudes)
    spread = [shift_by(piece, "y", s) for s, piece in enumerate(packed)]
    spread, slabs[0] = lax.optimization_barrier((spread, slabs[0]))
    spread = jnp.stack(spread)
    sent = [row_forward(table, 0, scalars, slabs[0])]
    fields = [lax.all_to_all(sent[0], plane, 0, 0, tiled=True)]

    def to_planes(rows, first, last):
        cut = [lax.dynamic_slice_in_dim(rows[:, first:last], lax.rem(y - zh - t + 8, 4), 1, 0)[0] for t in range(4)]
        return [shift_by(piece, "zh", t) for t, piece in enumerate(cut)]

    early = to_planes(spread, 0, EARLY)
    spread, slabs[-1] = lax.optimization_barrier((spread, slabs[-1]))
    late = to_planes(spread, EARLY, N // 2)
    slabs[-1], fields[0], early = lax.optimization_barrier((slabs[-1], fields[0], early))
    packed = [jnp.stack(pieces).reshape(4, -1, SUB, 128) for pieces in (early, late)]
    forward_lead = column_tables(table, "forward")
    inverse_lead = column_tables(table, "inverse")
    sent.extend(row_forward(table, c * count, scalars, slabs[c]) for c in range(1, CHUNKS))
    fields.extend(lax.all_to_all(piece, plane, 0, 0, tiled=True) for piece in sent[1:])
    returned, loss = columns(table, fields, zh[None].astype(jnp.int32), packed, forward_lead, inverse_lead)
    loss_total = jnp.sum(loss).reshape(1)
    for axis, distance in (("zl", 1), ("zh", 1), ("zh", 2)):
        loss_total = fold(loss_total, axis, distance)
    pieces = []
    returned = list(returned)
    for c in range(CHUNKS):
        back = lax.all_to_all(returned[c], plane, 0, 0, tiled=True)
        if c == 0:
            loss_total, back, returned[1:] = lax.optimization_barrier((loss_total, back, returned[1:]))
        term = row_inverse(table, c * count, scalars, back)
        if c == CHUNKS - 1:
            loss_total, term = lax.optimization_barrier((loss_total, term))
        pieces.append(lax.psum_scatter(term, ("zh", "zl"), scatter_dimension=0, tiled=False))
    for axis, distance in (("core", 1), ("x", 1), ("x", 2), ("y", 1), ("y", 2)):
        loss_total = fold(loss_total, axis, distance)
    gradient = jnp.concatenate(pieces, axis=1).astype(F32).reshape(2, SLAB, N)
    return gradient, loss_total[0] / (8 * N * N)


def solution(mesh):
    fine = Mesh(mesh.devices.reshape(4, 4, 2, 2, 4), ("x", "zh", "core", "zl", "y"))
    rows, mask = ("x", "zh", "core"), ("zl", "y")
    return jax.shard_map(
        functools.partial(shards, tables()),
        mesh=fine,
        in_specs=(P(None, rows + mask, None), P(mask, None, rows), P(mask)),
        out_specs=(P(None, rows + mask, None), P()),
        check_vma=False,
    )
```

```python
import functools
import math

import jax
import jax.numpy as jnp
import ml_dtypes
import numpy as np
from jax import lax
from jax.experimental import pallas as pl
from jax.experimental.pallas import tpu as pltpu
from jax.sharding import Mesh
from jax.sharding import PartitionSpec as P

N = 8192
LEAD = 64
SUB = 128
SLAB = 32
STRIDE = 136
EPSILON = 0.25
CHUNKS = 2
EARLY = 1280
BLOCK = 4
ROW_PRIME, COLUMN_PRIME, MASK_PRIME, MIX_PRIME = 73856093, 19349663, 83492791, 1274126177
BF16 = jnp.bfloat16
F32 = jnp.float32


def rounded(values):
    return values.astype(ml_dtypes.bfloat16).astype(np.float32)


def unit_table(outputs, inputs, length, direction):
    angles = (outputs[:, None] * inputs[None, :] % length) * (2.0 * math.pi / length)
    return np.cos(angles), direction * np.sin(angles)


def block_form(real_part, imag_part):
    return np.block([[real_part, -imag_part], [imag_part, real_part]])


def orders():
    x, core, jh, b = np.meshgrid(np.arange(4), np.arange(2), np.arange(2), np.arange(4), indexing="ij")
    k1 = (x * 16 + b * 4 + core * 2 + jh).reshape(-1)
    x, core, zh, zl = np.meshgrid(np.arange(4), np.arange(2), np.arange(4), np.arange(2), indexing="ij")
    n1 = (x * 16 + zh * 4 + core * 2 + zl).reshape(-1)
    return k1, n1


def tables():
    k1_order, n1_order = orders()
    lead, sub = np.arange(LEAD), np.arange(SUB)
    out = {}
    lanes = np.arange(256)
    half, part, low = lanes // 128, (lanes // 64) % 2, lanes % 64
    split = part * 128 + half * 64 + low
    for name, direction in (("forward", -1.0), ("inverse", 1.0)):
        sub_full = block_form(*map(rounded, unit_table(sub, sub, SUB, direction)))
        out[name + "_sub"] = sub_full.astype(ml_dtypes.bfloat16)
        if name == "forward":
            row_lead = block_form(*map(rounded, unit_table(k1_order, lead, LEAD, direction)))
            row_sub = sub_full.T[:, split]
            turn = unit_table(k1_order, sub, N, direction)
            col = tuple(map(rounded, unit_table(lead, n1_order, LEAD, direction)))
        else:
            row_lead = block_form(*map(rounded, unit_table(lead, k1_order, LEAD, direction)))
            row_sub = sub_full.T[split, :]
            turn = tuple(np.repeat(t, 8, axis=0) for t in unit_table(k1_order, sub, N, direction))
            col = tuple(map(rounded, unit_table(n1_order, lead, LEAD, direction)))
        out[name + "_row_lead"] = row_lead.astype(ml_dtypes.bfloat16)
        out[name + "_row_sub"] = row_sub.astype(ml_dtypes.bfloat16)
        out[name + "_turn"] = np.stack(turn).astype(np.float32)
        col_plain = block_form(*col).astype(np.float32)
        col_quarter = block_form(-col[1], col[0]).astype(np.float32)
        out[name + "_col"] = np.stack([col_plain, col_quarter])
        twist = unit_table(sub, np.concatenate([lead, lead]), N, direction)
        out[name + "_col_turn"] = np.stack(twist).astype(np.float32)
    return out


def column_tables(table, name):
    plain, quarter = table[name + "_col"]
    cosine, sine = table[name + "_col_turn"]
    plain, quarter, cosine, sine = map(jnp.asarray, (plain, quarter, cosine, sine))
    if name == "forward":
        cosine, sine = cosine[:, :, None], sine[:, :, None]
    else:
        cosine, sine = cosine[:, None, :], sine[:, None, :]
    return (plain[None] * cosine + quarter[None] * sine).astype(BF16)


def phase_code(hashed_columns, row_term):
    mixed = hashed_columns ^ row_term
    mixed = mixed ^ lax.shift_right_logical(mixed, jnp.int32(13))
    mixed = mixed * jnp.int32(MIX_PRIME)
    mixed = mixed ^ lax.shift_right_logical(mixed, jnp.int32(16))
    return lax.shift_right_logical(mixed, jnp.int32(28))


def column_hash():
    shape = (LEAD, SUB)
    column = lax.broadcasted_iota(jnp.int32, shape, 0) * SUB + lax.broadcasted_iota(jnp.int32, shape, 1)
    return column * jnp.int32(COLUMN_PRIME)


def quarter_turn(real_part, imag_part, code, forward):
    odd = (code & 1) == 1
    first = jnp.where(odd, imag_part, real_part)
    second = jnp.where(odd, real_part, imag_part)
    high = (code & 2) == 2
    mixed = ((code ^ lax.shift_right_logical(code, jnp.int32(1))) & 1) == 1
    flip_real, flip_imag = (mixed, high) if forward else (high, mixed)
    return jnp.where(flip_real, -first, first), jnp.where(flip_imag, -second, second)


def row_forward_kernel(first_row, scalars, image, lead_table, sub_table, turn, out, swap):
    columns = column_hash()
    block_row = first_row + pl.program_id(0) * BLOCK

    def body(r, carry):
        stacked = []
        for zs in range(8):
            row = scalars[zs] + block_row + r
            code = phase_code(columns, (row * jnp.int32(ROW_PRIME)) ^ scalars[8])
            real_part, imag_part = image[zs, 0, r].astype(F32), image[zs, 1, r].astype(F32)
            real_part, imag_part = quarter_turn(real_part, imag_part, code, True)
            stacked.append(jnp.concatenate([real_part, imag_part], axis=0).astype(BF16))
        first = jnp.dot(lead_table[...], jnp.concatenate(stacked, axis=1), preferred_element_type=F32)
        cosine, sine = turn[0], turn[1]
        middle = []
        for zs in range(8):
            real_part, imag_part = first[:LEAD, zs * 128 : zs * 128 + 128], first[LEAD:, zs * 128 : zs * 128 + 128]
            turned = [real_part * cosine - imag_part * sine, real_part * sine + imag_part * cosine]
            middle.append(jnp.concatenate(turned, axis=1).astype(BF16))
        second = jnp.dot(jnp.concatenate(middle, axis=0), sub_table[...], preferred_element_type=F32)
        for zs in range(8):
            for half in range(2):
                swap[half, pl.ds(zs, LEAD, stride=8), :] = second[zs * LEAD : (zs + 1) * LEAD, half * 128 : half * 128 + 128]
        for x in range(4):
            for core in range(2):
                for jh in range(2):
                    at = ((x * 2 + core) * 2 + jh) * 32
                    for half in range(2):
                        out[(x * 4 + jh * 2 + half) * 2 + core, r] = swap[half, at : at + 32, :].astype(BF16)
        return carry

    lax.fori_loop(0, BLOCK, body, 0, unroll=True)


def row_inverse_kernel(first_row, scalars, field, lead_table, sub_table, turn, out, swap):
    columns = column_hash()
    block_row = first_row + pl.program_id(0) * BLOCK

    def body(r, carry):
        blocks = []
        for x in range(4):
            for core in range(2):
                for jh in range(2):
                    pair = [field[(x * 4 + jh * 2 + half) * 2 + core, r] for half in range(2)]
                    blocks.append(jnp.concatenate(pair, axis=1))
        first = jnp.dot(jnp.concatenate(blocks, axis=0), sub_table[...], preferred_element_type=F32)
        real_part, imag_part = first[:, :128], first[:, 128:]
        cosine, sine = turn[0], turn[1]
        swap[0] = real_part * cosine - imag_part * sine
        swap[1] = real_part * sine + imag_part * cosine
        middle = []
        for zs in range(8):
            parts = [swap[part, pl.ds(zs, LEAD, stride=8), :] for part in range(2)]
            middle.append(jnp.concatenate(parts, axis=0).astype(BF16))
        second = jnp.dot(lead_table[...], jnp.concatenate(middle, axis=1), preferred_element_type=F32)
        second = second * (1.0 / N)
        for zs in range(8):
            row = scalars[zs] + block_row + r
            code = phase_code(columns, (row * jnp.int32(ROW_PRIME)) ^ scalars[8])
            real_part, imag_part = second[:LEAD, zs * 128 : zs * 128 + 128], second[LEAD:, zs * 128 : zs * 128 + 128]
            real_part, imag_part = quarter_turn(real_part, imag_part, code, False)
            out[zs, 0, r] = real_part.astype(BF16)
            out[zs, 1, r] = imag_part.astype(BF16)
        return carry

    lax.fori_loop(0, BLOCK, body, 0, unroll=True)


def pair_up(first, second, low):
    return jnp.where(low, first, pltpu.roll(second, 64, 1)), jnp.where(low, pltpu.roll(first, 64, 1), second)


def pack_kernel(place, amplitudes, *outs):
    for shift, out in enumerate(outs):
        piece = lax.rem(place[0] + shift, 4)
        lanes = pl.ds(pl.multiple_of(piece // 2 * 128, 128), 128)
        upper, lower = amplitudes[0, :, lanes].astype(F32), amplitudes[1, :, lanes].astype(F32)
        low = lax.broadcasted_iota(jnp.int32, upper.shape, 1) < 64
        left, right = pair_up(upper, lower, low)
        out[...] = jnp.where(lax.rem(piece, 2) == 0, left, right).astype(BF16)


def column_kernel(*refs):
    fields = refs[:CHUNKS]
    place, pieces = refs[CHUNKS], refs[CHUNKS + 1 : CHUNKS + 9]
    forward_lead, inverse_lead, forward_sub, inverse_sub = refs[CHUNKS + 9 : CHUNKS + 13]
    outs = refs[CHUNKS + 13 : 2 * CHUNKS + 13]
    loss, hold = refs[2 * CHUNKS + 13 : 2 * CHUNKS + 15]
    buffers, sems, piece_sems = refs[2 * CHUNKS + 15 : -2], refs[-2], refs[-1]
    count = SLAB // CHUNKS

    early, late = buffers[-2:]
    operands = list(fields) + [forward_lead, inverse_lead]
    loads = [pltpu.make_async_copy(operand, buffers[n], sems.at[n]) for n, operand in enumerate(operands)]
    amplitude_loads = [
        pltpu.make_async_copy(piece, (early, late)[n // 4].at[n % 4], piece_sems.at[n]) for n, piece in enumerate(pieces)
    ]
    for n in [0, CHUNKS] + list(range(1, CHUNKS)):
        loads[n].start()
    for load in amplitude_loads:
        load.start()
    loads[CHUNKS + 1].start()
    fields = buffers[:CHUNKS]
    forward_lead, inverse_lead = buffers[CHUNKS : CHUNKS + 2]
    stores = [pltpu.make_async_copy(buffers[CHUNKS + 2 + n], outs[n], sems.at[CHUNKS + 2 + n]) for n in range(CHUNKS)]
    outs = buffers[CHUNKS + 2 : 2 * CHUNKS + 2]
    loads[CHUNKS].wait()

    for chunk in range(CHUNKS):
        loads[chunk].wait()

        def forward(step, carry, chunk=chunk):
            y, r = step // count, lax.rem(step, count)
            at = y * SLAB + chunk * count + r
            low = lax.broadcasted_iota(jnp.int32, (8, 128), 1) < 64
            parts = [[[], []], [[], []]]
            for x in range(4):
                for core in range(2):
                    block = fields[chunk][(x * 4 + y) * 2 + core, r].astype(F32)
                    for pair in range(2):
                        real_part, imag_part = pair_up(block[pair * 16 : pair * 16 + 8], block[pair * 16 + 8 : pair * 16 + 16], low)
                        parts[0][pair].append(real_part)
                        parts[1][pair].append(imag_part)
            stacked = jnp.concatenate(
                [jnp.concatenate([jnp.concatenate(parts[part][pair], axis=0) for pair in range(2)], axis=1) for part in range(2)], axis=0
            ).astype(BF16)
            result = jnp.dot(forward_lead[at], stacked, preferred_element_type=F32)
            for part in range(2):
                for pair in range(2):
                    hold[part, pair, pl.ds(at, LEAD, stride=STRIDE), :] = result[part * 64 : part * 64 + 64, pair * 128 : pair * 128 + 128]
            return carry

        lax.fori_loop(0, 4 * count, forward, 0, unroll=8)

    loss[...] = jnp.zeros_like(loss)
    for load in amplitude_loads:
        load.wait()

    def middle(amplitudes, first_k1, index, carry):
        k1_low = first_k1 + index
        low = lax.broadcasted_iota(jnp.int32, (SUB, 128), 1) < 64
        measured = [[], []]
        for pair in range(2):
            first, second = (amplitudes[lax.rem(place[0] + 4 - b, 4), index].astype(F32) for b in (pair * 2, pair * 2 + 1))
            for high, values in enumerate(pair_up(first, second, low)):
                measured[high].append(values)
        places = [pl.ds(pl.multiple_of((k1_low + high * 32) * STRIDE, 8), SUB) for high in range(2)]
        stacked = [
            jnp.concatenate(
                [jnp.concatenate([hold[part, pair, at, :].astype(BF16) for pair in range(2)], axis=1) for part in range(2)], axis=0
            )
            for at in places
        ]
        spectra = [jnp.dot(forward_sub[...], values, preferred_element_type=F32) for values in stacked]
        weighted, total = [], 0.0
        for spectrum, values in zip(spectra, measured):
            real_part, imag_part = spectrum[:SUB] * (1.0 / N), spectrum[SUB:] * (1.0 / N)
            amplitude = jnp.concatenate(values, axis=1)
            squared = real_part * real_part + imag_part * imag_part + EPSILON
            inverse = lax.rsqrt(squared)
            kept = 1.0 - amplitude * inverse
            misfit = squared * inverse - amplitude
            total = total + jnp.sum((misfit * misfit).reshape(SUB // 8, 8, 256), axis=0)
            weighted.append(jnp.concatenate([(real_part * kept).astype(BF16), (imag_part * kept).astype(BF16)], axis=0))
        results = [jnp.dot(inverse_sub[...], values, preferred_element_type=F32) for values in weighted]
        loss[...] += total
        for at, result in zip(places, results):
            for part in range(2):
                for pair in range(2):
                    hold[part, pair, at, :] = result[part * SUB : part * SUB + SUB, pair * 128 : pair * 128 + 128]
        return carry

    lax.fori_loop(0, EARLY // SUB, functools.partial(middle, early, 0), 0, unroll=2)
    lax.fori_loop(0, 32 - EARLY // SUB, functools.partial(middle, late, EARLY // SUB), 0, unroll=2)

    loads[CHUNKS + 1].wait()
    for chunk in range(CHUNKS):

        def inverse(step, carry, chunk=chunk):
            y, r = step // count, lax.rem(step, count)
            at = y * SLAB + chunk * count + r
            low = lax.broadcasted_iota(jnp.int32, (8, 128), 1) < 64
            stacked = jnp.concatenate(
                [jnp.concatenate([hold[part, pair, pl.ds(at, LEAD, stride=STRIDE), :] for pair in range(2)], axis=1) for part in range(2)],
                axis=0,
            ).astype(BF16)
            result = jnp.dot(inverse_lead[at], stacked, preferred_element_type=F32)
            for x in range(4):
                for core in range(2):
                    row = (x * 2 + core) * 8
                    block = []
                    for pair in range(2):
                        real_part = result[row : row + 8, pair * 128 : pair * 128 + 128]
                        imag_part = result[64 + row : 64 + row + 8, pair * 128 : pair * 128 + 128]
                        block.extend(pair_up(real_part, imag_part, low))
                    outs[chunk][(x * 4 + y) * 2 + core, r] = jnp.concatenate(block, axis=0).astype(BF16)
            return carry

        lax.fori_loop(0, 4 * count, inverse, 0, unroll=8)
        stores[chunk].start()

    for store in stores:
        store.wait()


VMEM = pl.BlockSpec(memory_space=pltpu.VMEM)
ANY = pl.BlockSpec(memory_space=pl.ANY)
SMEM = pl.BlockSpec(memory_space=pltpu.SMEM)


def params(mib):
    return pltpu.CompilerParams(vmem_limit_bytes=mib * 2**20)


def cost(flops, moved):
    return pl.CostEstimate(flops=flops, bytes_accessed=moved, transcendentals=0)


def whole(array):
    return pl.BlockSpec(array.shape, lambda i: (0,) * array.ndim, pipeline_mode=pl.Buffered(1))


def row_forward(table, first_row, scalars, image):
    count = image.shape[2]
    constants = [table["forward_row_lead"], table["forward_row_sub"], table["forward_turn"]]
    return pl.pallas_call(
        functools.partial(row_forward_kernel, first_row),
        grid=(count // BLOCK,),
        out_shape=jax.ShapeDtypeStruct((32, count, 32, 128), BF16),
        in_specs=[SMEM, pl.BlockSpec((8, 2, BLOCK, LEAD, SUB), lambda i: (0, 0, i, 0, 0))] + [whole(c) for c in constants],
        out_specs=pl.BlockSpec((32, BLOCK, 32, 128), lambda i: (0, i, 0, 0)),
        scratch_shapes=[pltpu.VMEM((2, 512, 128), F32)],
        compiler_params=params(58),
        cost_estimate=cost(count * 10**9, count * 2**19),
        name="row_forward",
    )(scalars, image, *constants)


def row_inverse(table, first_row, scalars, field):
    count = field.shape[1]
    constants = [table["inverse_row_lead"], table["inverse_row_sub"], table["inverse_turn"]]
    return pl.pallas_call(
        functools.partial(row_inverse_kernel, first_row),
        grid=(count // BLOCK,),
        out_shape=jax.ShapeDtypeStruct((8, 2, count, LEAD, SUB), BF16),
        in_specs=[SMEM, pl.BlockSpec((32, BLOCK, 32, 128), lambda i: (0, i, 0, 0))] + [whole(c) for c in constants],
        out_specs=pl.BlockSpec((8, 2, BLOCK, LEAD, SUB), lambda i: (0, 0, i, 0, 0)),
        scratch_shapes=[pltpu.VMEM((2, 512, 128), F32)],
        compiler_params=params(58),
        cost_estimate=cost(count * 10**9, count * 2**19),
        name="row_inverse",
    )(scalars, field, *constants)


def pack(place, amplitudes):
    rows = N // 2
    step = 512
    return pl.pallas_call(
        pack_kernel,
        grid=(rows // step,),
        out_shape=[jax.ShapeDtypeStruct((rows, 128), BF16)] * 4,
        in_specs=[SMEM, pl.BlockSpec((2, step, 256), lambda i: (0, i, 0))],
        out_specs=[pl.BlockSpec((step, 128), lambda i: (i, 0))] * 4,
        cost_estimate=cost(10**7, 2**23),
        name="pack",
    )(place, amplitudes.reshape(2, rows, 256))


def columns(table, fields, place, amplitudes, forward_lead, inverse_lead):
    count = SLAB // CHUNKS
    pieces = [piece for group in amplitudes for piece in group]
    moved = list(fields) + [forward_lead, inverse_lead]
    together = [pltpu.VMEM((4,) + group[0].shape, BF16) for group in amplitudes]
    out = jax.ShapeDtypeStruct((32, count, 32, 128), BF16)
    result = pl.pallas_call(
        column_kernel,
        out_shape=[out] * CHUNKS + [jax.ShapeDtypeStruct((8, 256), F32)],
        in_specs=[ANY] * CHUNKS + [SMEM] + [ANY] * 10 + [VMEM] * 2,
        out_specs=[ANY] * CHUNKS + [VMEM],
        scratch_shapes=[pltpu.VMEM((2, 2, LEAD * STRIDE, 128), F32)]
        + [pltpu.VMEM(array.shape, BF16) for array in moved + [out] * CHUNKS]
        + together
        + [pltpu.SemaphoreType.DMA((2 * CHUNKS + 2,)), pltpu.SemaphoreType.DMA((8,))],
        compiler_params=params(58),
        cost_estimate=cost(40 * 10**9, 2**25),
        name="columns",
    )(*fields, place, *pieces, forward_lead, inverse_lead, table["forward_sub"], table["inverse_sub"])
    return result[:-1], result[-1]


def shift_by(piece, axis, shift):
    return piece if shift == 0 else lax.ppermute(piece, axis, [(i, (i + shift) % 4) for i in range(4)])


def fold(value, axis, distance):
    return value + lax.ppermute(value, axis, [(i, i ^ distance) for i in range(lax.axis_size(axis))])


def shards(table, image_field, amplitudes, mask_ids):
    plane = ("x", "y", "core")
    x, zh, core, zl, y = (lax.axis_index(name) for name in ("x", "zh", "core", "zl", "y"))
    swap = [(a * 4 + b, b * 4 + a) for a in range(4) for b in range(4)]
    mask_term = (lax.ppermute(mask_ids, ("zh", "y"), swap) + 1) * jnp.int32(MASK_PRIME)
    zs = jnp.arange(8, dtype=jnp.int32)
    first_rows = (((x * 4 + zs // 2) * 2 + core) * 8 + zs % 2 * 4 + y) * SLAB
    scalars = jnp.concatenate([first_rows.astype(jnp.int32), mask_term])
    count = SLAB // CHUNKS

    image = image_field.reshape(2, SLAB, LEAD, SUB)
    slabs = [lax.all_gather(image[:, c * count : (c + 1) * count], ("zh", "zl"), axis=0) for c in range(CHUNKS)]

    packed = pack(y[None].astype(jnp.int32), amplitudes)
    spread = [shift_by(piece, "y", s) for s, piece in enumerate(packed)]
    spread, slabs[0] = lax.optimization_barrier((spread, slabs[0]))
    spread = jnp.stack(spread)
    sent = [row_forward(table, 0, scalars, slabs[0])]
    fields = [lax.all_to_all(sent[0], plane, 0, 0, tiled=True)]

    def to_planes(rows, first, last):
        cut = [lax.dynamic_slice_in_dim(rows[:, first:last], lax.rem(y - zh - t + 8, 4), 1, 0)[0] for t in range(4)]
        return [shift_by(piece, "zh", t) for t, piece in enumerate(cut)]

    early = to_planes(spread, 0, EARLY)
    spread, slabs[-1] = lax.optimization_barrier((spread, slabs[-1]))
    late = to_planes(spread, EARLY, N // 2)
    slabs[-1], fields[0], early = lax.optimization_barrier((slabs[-1], fields[0], early))
    packed = [[piece.reshape(-1, SUB, 128) for piece in pieces] for pieces in (early, late)]
    forward_lead = column_tables(table, "forward")
    inverse_lead = column_tables(table, "inverse")
    sent.extend(row_forward(table, c * count, scalars, slabs[c]) for c in range(1, CHUNKS))
    fields.extend(lax.all_to_all(piece, plane, 0, 0, tiled=True) for piece in sent[1:])
    returned, loss = columns(table, fields, zh[None].astype(jnp.int32), packed, forward_lead, inverse_lead)
    loss_total = jnp.sum(loss).reshape(1)
    for axis, distance in (("zl", 1), ("zh", 1), ("zh", 2)):
        loss_total = fold(loss_total, axis, distance)
    pieces = []
    returned = list(returned)
    for c in range(CHUNKS):
        back = lax.all_to_all(returned[c], plane, 0, 0, tiled=True)
        if c == 0:
            loss_total, back, returned[1:] = lax.optimization_barrier((loss_total, back, returned[1:]))
        term = row_inverse(table, c * count, scalars, back)
        if c == CHUNKS - 1:
            loss_total, term = lax.optimization_barrier((loss_total, term))
        pieces.append(lax.psum_scatter(term, ("zh", "zl"), scatter_dimension=0, tiled=False))
    for axis, distance in (("core", 1), ("x", 1), ("x", 2), ("y", 1), ("y", 2)):
        loss_total = fold(loss_total, axis, distance)
    gradient = jnp.concatenate(pieces, axis=1).astype(F32).reshape(2, SLAB, N)
    return gradient, loss_total[0] / (8 * N * N)


def solution(mesh):
    fine = Mesh(mesh.devices.reshape(4, 4, 2, 2, 4), ("x", "zh", "core", "zl", "y"))
    rows, mask = ("x", "zh", "core"), ("zl", "y")
    return jax.shard_map(
        functools.partial(shards, tables()),
        mesh=fine,
        in_specs=(P(None, rows + mask, None), P(mask, None, rows), P(mask)),
        out_specs=(P(None, rows + mask, None), P()),
        check_vma=False,
    )
```
